32 devices in a mesh: bulk: 4 (over z), expert: 8 (over y, x, core).
Axes of the slice: x: 2, y: 2, z: 4, core: 2. Of those that a mesh axis runs over, the one named last changes fastest.
Arguments:
- tokens: bfloat16 [2048, 7168], P(('bulk', 'expert')), may hold values from -6 to 6
- expert_ids: int32 [2048, 8], P(('bulk', 'expert')), may hold values from 0 to 255, all different within a row; in each aligned block of 64 rows (0 to 63, 64 to 127, ...) at most 3 rows name the same one
- gate_values: float32 [2048, 8], P(('bulk', 'expert')), may hold values from 0.25 to 2.5
- placement: int32 [8], replicated, may hold values from 0 to 7, as said below
- gate_weight: bfloat16 [8, 7168, 2048], P('expert', 'bulk'), may hold values from -0.0625 to 0.0625
- up_weight: bfloat16 [8, 7168, 2048], P('expert', 'bulk'), may hold values from -0.0625 to 0.0625
- down_weight: bfloat16 [8, 2048, 7168], P('expert', None, 'bulk'), may hold values from -0.125 to 0.125
Outputs:
- layer_out: bfloat16 [2048, 7168], P(('bulk', 'expert'))
- host_load: int32 [32, 8], P(('bulk', 'expert'))
The draws below stay inside these ranges and needn't reach their ends.
Inputs may be any that keep to these rules, and one draw needn't show every extreme that they name: `expert_ids`: in each aligned block of 64 rows (the tokens of one device) no expert is named by more than 3 rows; a token names an expert at most once. Exactly one expert e has placement[e] != e: its home device e is power-capped and its host is the next device of the expert axis, placement[e] = (e + 1) mod 8; every other expert stays on its home device.
All inputs are finite; a program needn't handle non-finite values.
Results may differ from the reference program's by a relative error of at most 0.018.
Values may be sent and summed in bfloat16 or wider, within the bound.
A program may use at most 128 MiB of HBM per device.

```python
import math
import jax
import jax.numpy as jnp
import numpy as np
from jax import lax

D = 7168
FF = 2048
EXPERTS = 256
TOP = 8
TOK_DEV = 64
CAP = 3
IN_FLIGHT = 8
SOURCES = 32
TOKENS = 2048
N_BULK = 4


def draw_placement(key, part):
    home_device = jnp.arange(IN_FLIGHT, dtype=jnp.int32)
    removed_device = jax.random.randint(jax.random.fold_in(key, 11), (), 0, IN_FLIGHT)
    host_device = (removed_device + 1) % IN_FLIGHT
    return jnp.where(home_device == removed_device, host_device, home_device).astype(jnp.int32)


def steps_of(rng, shape, cuts, least, top_value):
    loudness = 1.0
    for axis_at, parts in cuts:
        draws = jax.random.uniform(jax.random.fold_in(jax.random.fold_in(rng, 6), axis_at), (parts,), jnp.float32, least / len(cuts), top_value / len(cuts))
        loudness = loudness * jnp.repeat(jnp.exp(draws), shape[axis_at] // parts).reshape((-1,) + (1,) * (len(shape) - 1 - axis_at))
    return loudness


def deal_out(own_key, own, number, rows, count, top, limit, lean):
    ranking = jax.random.permutation(own_key, count)
    packed, ordinary = portions_of(count, rows * top, limit, lean, True), portions_of(count, rows * top, limit, lean, False)
    places = jnp.arange(count)

    def named(tallies, offset_by):
        used = int((tallies > 0).sum())
        fixed = max(1, used // 4)
        moved = fixed + (places - fixed + offset_by * (used - fixed)) % max(1, count - fixed)
        return jnp.zeros((count,), jnp.int32).at[ranking[jnp.where(places < fixed, places, moved)]].set(jnp.asarray(tallies, jnp.int32))

    tallies = jnp.where(number % 4 == 0, named(packed, number // 4), named(ordinary, number - number // 4 - 1))
    mixed = jax.random.permutation(jax.random.fold_in(own, 3), count)
    giver, receiver = mixed[0:count // 2 * 2:2], mixed[1:count // 2 * 2:2]
    margin = jnp.minimum(tallies[giver] - 1, limit - tallies[receiver]) // 2
    margin = jnp.where((giver == ranking[0]) | (receiver == ranking[0]) | (tallies[receiver] == 0), 0, jnp.maximum(margin, 0))
    moved = jax.random.randint(jax.random.fold_in(own, 4), (count // 2,), 0, 1 << 20) % (margin + 1)
    tallies = tallies.at[giver].add(-moved).at[receiver].add(moved)
    labels = jnp.searchsorted(jnp.cumsum(tallies), jnp.arange(rows * top), side="right").astype(jnp.int32)
    table = labels.reshape(top, rows).T
    table = table[jax.random.permutation(jax.random.fold_in(own, 1), rows)]
    offset_by = jax.random.randint(jax.random.fold_in(own, 2), (rows, 1), 0, top)
    return jnp.take_along_axis(table, (jnp.arange(top)[None, :] + offset_by) % top, axis=1)


def portions_of(count, total, reach, skew, full):
    portions = [(1 << 20) // math.isqrt(standing ** skew) + 1 for standing in range(1, count + 1)]
    largest = reach if full else min(reach, max(-(-total // count), total * portions[0] // sum(portions)))
    least = 1 if total - largest >= count - 1 else 0
    counts, spare = [largest] + [least] * (count - 1), total - largest - least * (count - 1)
    while spare > 0:
        free = [i for i in range(1, count) if counts[i] < largest] or [i for i in range(1, count) if counts[i] < reach]
        pool, remaining = sum([portions[i] for i in free]), spare
        for i in free:
            more = min(reach - counts[i], max(1, remaining * portions[i] // pool), spare)
            counts[i] = counts[i] + more
            spare = spare - more
    return np.array(counts)


def bell_draw(stream_key, extent, spread, reach, cuts=(), held_as=jnp.bfloat16):
    values = spread * jax.random.normal(stream_key, extent, jnp.float32)
    if cuts:
        values = values * steps_of(stream_key, extent, cuts, -0.22, 0.18)
    return jnp.clip(values, -reach, reach).astype(held_as)


def setup_inputs(seed: int = 0) -> dict:
    key_of = jax.random.split(jax.random.key(seed), 8)
    tokens = bell_draw(key_of[0], (TOKENS, D), 1.0, 6.0, ((0, 32),))
    expert_ids_keys = jax.random.split(jax.random.fold_in(key_of[1], 1), TOKENS // TOK_DEV)
    expert_ids_turns = jax.random.permutation(jax.random.fold_in(key_of[1], 3), TOKENS // TOK_DEV)
    expert_ids = jax.vmap(lambda own, number: deal_out(jax.random.fold_in(key_of[1], 2), own, number, TOK_DEV, EXPERTS, TOP, CAP, 1))(expert_ids_keys, expert_ids_turns).reshape((TOKENS, TOP))
    gate_values = jnp.clip(0.25 + 2.25 * jax.random.uniform(key_of[2], (TOKENS, TOP), jnp.float32) ** steps_of(key_of[2], (TOKENS, TOP), ((0, 32),), -0.2, 0.2), 0.25, 2.5)
    placement = draw_placement(jax.random.fold_in(key_of[7], 71), 0)
    gate_weight = bell_draw(key_of[4], (IN_FLIGHT, D, FF), D ** -0.5, 0.0625, ((0, 8), (1, 4)))
    up_weight = bell_draw(key_of[5], (IN_FLIGHT, D, FF), D ** -0.5, 0.0625, ((0, 8), (1, 4)))
    down_weight = bell_draw(key_of[6], (IN_FLIGHT, FF, D), FF ** -0.5, 0.125, ((0, 8), (2, 4)))
    return {"tokens": tokens, "expert_ids": expert_ids, "gate_values": gate_values, "placement": placement, "gate_weight": gate_weight, "up_weight": up_weight, "down_weight": down_weight}


def reference(tokens, expert_ids, gate_values, placement, gate_weight, up_weight, down_weight):
    slice_width = D // N_BULK
    bound = SOURCES * CAP

    def step(running, inputs_now):
        expert, w_gate_now, w_up_now, w_down_now = inputs_now
        is_named_pair = expert_ids == expert
        is_named = jnp.any(is_named_pair, axis=1)
        pair_weight = jnp.sum(jnp.where(is_named_pair, gate_values, 0.0), axis=1)
        row_index = jnp.nonzero(is_named, size=bound, fill_value=0)[0].astype(jnp.int32)
        is_valid = jnp.arange(bound, dtype=jnp.int32) < jnp.sum(is_named.astype(jnp.int32))
        features = tokens[row_index].astype(jnp.float32).reshape(bound, N_BULK, slice_width)
        gate_blocks = jnp.einsum("nbd,bdf->nbf", features, w_gate_now.astype(jnp.float32).reshape(N_BULK, slice_width, FF))
        up_blocks = jnp.einsum("nbd,bdf->nbf", features, w_up_now.astype(jnp.float32).reshape(N_BULK, slice_width, FF))
        gate_rounded = lax.optimization_barrier(gate_blocks.astype(jnp.bfloat16))
        up_rounded = lax.optimization_barrier(up_blocks.astype(jnp.bfloat16))
        gate_sum = jnp.sum(gate_rounded.astype(jnp.float32), axis=1)
        up_sum = jnp.sum(up_rounded.astype(jnp.float32), axis=1)
        hidden = (jax.nn.silu(gate_sum) * up_sum).astype(jnp.bfloat16)
        expert_out = jnp.dot(hidden, w_down_now, preferred_element_type=jnp.float32).astype(jnp.bfloat16)
        pair_scale = jnp.where(is_valid, pair_weight[row_index], 0.0)
        running = running.at[row_index].add(pair_scale[:, None] * expert_out.astype(jnp.float32))
        return running, None

    start_sum = jnp.zeros((TOKENS, D), jnp.float32)
    expert_range = jnp.arange(IN_FLIGHT, dtype=jnp.int32)
    running, _ = lax.scan(step, start_sum, (expert_range, gate_weight, up_weight, down_weight))
    layer_out = running.astype(jnp.bfloat16)

    block_ids = expert_ids.reshape(SOURCES, TOK_DEV * TOP)
    block_live = block_ids < IN_FLIGHT
    safe_ids = jnp.where(block_live, block_ids, 0)
    row_within = (jnp.arange(TOK_DEV * TOP, dtype=jnp.int32) // TOP)[None, :]
    replica = (safe_ids + 1) % IN_FLIGHT
    destination = jnp.where(row_within % 2 == 1, replica, placement[safe_ids]).astype(jnp.int32)
    matches = (destination[:, :, None] == expert_range[None, None, :]) & block_live[:, :, None]
    host_load = jnp.sum(matches.astype(jnp.int32), axis=1)
    return layer_out, host_load
```

```python
import functools

import jax
import jax.numpy as jnp
import ml_dtypes
import numpy as np
from jax import lax
from jax.experimental import pallas as pl
from jax.experimental.pallas import tpu as pltpu
from jax.sharding import PartitionSpec as P

CAP = 3
BF = jnp.bfloat16
F32 = jnp.float32
MESH = pl.DeviceIdType.MESH


def dot(a, b):
    return jnp.dot(a, b, preferred_element_type=F32)


def kernel(
    B, E, RP, H, G, tok_hbm, ids, gv, place, p1, p1t, p2, p2t, wg_hbm, wu_hbm, wd_hbm,
    fin, cs, ld, tok, wgu, wd, og, oin, xs, xr, x, pout, pin, hin, acc, back, rb, csv, ldv,
    tsem, csem, fsem, wsem, dsem, s1, r1, s2, r2, s3, r3, s4, r4, s5, r5, s6, r6,
):
    TOP, T = ids.shape
    SL = E * CAP
    DS = wg_hbm.shape[1]
    FB = wg_hbm.shape[2] // B
    DH = DS // H
    FH = FB // G
    mb = lax.axis_index("bulk")
    me = lax.axis_index("expert")

    def bulk_at(k):
        return lax.rem(mb + k + B, B)

    def expert_at(k):
        return lax.rem(me + k + E, E)

    def down_copy(k):
        rows = pl.ds(pl.multiple_of(bulk_at(-k) * FB, FB), FB)
        return pltpu.make_async_copy(wd_hbm.at[0, rows, :], wd.at[k], dsem.at[k])

    def up_copy(i, k, g):
        cols = pl.ds(pl.multiple_of(bulk_at(k) * FB + g * FH, FH), FH)
        return pltpu.make_async_copy(
            (wg_hbm, wu_hbm)[i].at[0, :, cols],
            wgu.at[k, g, :, i * FH : (i + 1) * FH],
            wsem.at[i, k, g],
        )

    tok_copy = pltpu.make_async_copy(tok_hbm, tok, tsem)
    tok_copy.start()
    far_first = [(i + B // 2 - 1) % (B - 1) + 1 for i in range(B - 1)]
    order = far_first + [0]
    barrier = pltpu.get_barrier_semaphore()
    for k in range(1, B):
        pl.semaphore_signal(barrier, inc=1, device_id=(bulk_at(k), me), device_id_type=MESH)
    for k in range(1, E):
        pl.semaphore_signal(barrier, inc=1, device_id=(mb, expert_at(k)), device_id_type=MESH)

    slot = lax.broadcasted_iota(jnp.int32, (SL, T), 0)
    slot_expert = lax.div(slot, CAP)
    slot_rank = slot - slot_expert * CAP
    named = jnp.zeros((SL, T), F32)
    gates = jnp.zeros((SL, T), F32)
    for j in range(TOP):
        hit = ids[j : j + 1, :] == slot_expert
        named = named + jnp.where(hit, 1.0, 0.0)
        gates = gates + jnp.where(hit, gv[j : j + 1, :], 0.0)
    t_row = lax.broadcasted_iota(jnp.int32, (T, T), 0)
    t_col = lax.broadcasted_iota(jnp.int32, (T, T), 1)
    before = jnp.where(t_row < t_col, 1.0, 0.0).astype(BF)
    rank = dot(named.astype(BF), before)
    chosen = jnp.where(rank == slot_rank.astype(F32), named, 0.0)
    selector = chosen.astype(BF)

    def send1(k, h):
        return pltpu.make_async_remote_copy(
            og.at[k, h], oin.at[k, h], s1.at[k, h], r1.at[k, h],
            device_id=(bulk_at(k), me), device_id_type=MESH,
        )

    pl.semaphore_wait(barrier, B + E - 2)
    tok_copy.wait()
    for h in range(H):
        for k in order:
            cols = pl.ds(pl.multiple_of(bulk_at(k) * DS + h * DH, 128), DH)
            rows = dot(selector, tok[:, cols]).astype(BF)
            if k:
                og[k, h] = rows
                send1(k, h).start()
            else:
                oin[0, h] = rows
    for k in order:
        for g in range(G):
            up_copy(0, k, g).start()
            up_copy(1, k, g).start()
    for k in range(B):
        down_copy(k).start()

    member = jnp.zeros((E, T), F32)
    e_iota = lax.broadcasted_iota(jnp.int32, (E, T), 0)
    for j in range(TOP):
        member = member + jnp.where(ids[j : j + 1, :] == e_iota, 1.0, 0.0)
    odd_t = lax.rem(lax.broadcasted_iota(jnp.int32, (8, T), 1), 2) == 1
    odd = jnp.where(odd_t, 1.0, 0.0).astype(BF)
    even = jnp.where(odd_t, 0.0, 1.0).astype(BF)
    er = lax.broadcasted_iota(jnp.int32, (E, E), 0)
    ec = lax.broadcasted_iota(jnp.int32, (E, E), 1)
    shift = jnp.where(er == lax.rem(ec + 1, E), 1.0, 0.0).astype(BF)
    home = jnp.where(er == place[...], 1.0, 0.0).astype(BF)

    def across(a, b):
        return lax.dot_general(a, b, (((1,), (1,)), ((), ())), preferred_element_type=F32)

    member = member.astype(BF)
    loads = across(across(odd, member).astype(BF), shift) + across(
        across(even, member).astype(BF), home
    )
    ldv[...] = loads
    eye = jnp.where(t_row == t_col, 1.0, 0.0).astype(BF)
    combine = chosen * gates
    c_hi = combine.astype(BF)
    c_rest = combine - c_hi.astype(F32)
    c_mid = c_rest.astype(BF)
    c_lo = (c_rest - c_mid.astype(F32)).astype(BF)
    for i, c in enumerate((c_hi, c_mid, c_lo)):
        csv[i] = across(eye, c).astype(BF)
    side = (
        pltpu.make_async_copy(csv, cs, csem.at[0]),
        pltpu.make_async_copy(ldv, ld, csem.at[1]),
    )
    for copy in side:
        copy.start()

    def block(k):
        return pl.ds(pl.multiple_of(k * RP, RP), RP)

    def send2(k, h):
        return pltpu.make_async_remote_copy(
            xs.at[h, block(expert_at(k))], xr.at[h, block(k)], s2.at[k, h], r2.at[k, h],
            device_id=(mb, expert_at(k)), device_id_type=MESH,
        )

    for h in range(H):
        rows = dot(p1[mb], oin[0, h])
        for k in range(1, B):
            send1(k, h).wait_recv()
            rows = rows + dot(p1[bulk_at(-k)], oin[k, h])
        xs[h] = rows.astype(BF)
        for k in range(1, E):
            send2(k, h).start()
        xr[h, 0:RP] = xs[h, block(me)]
    for h in range(H):
        for k in range(1, E):
            send2(k, h).wait_recv()
        x[:, h * DH : (h + 1) * DH] = dot(p2[...], xr[h]).astype(BF)

    pair = lax.div(mb, 2)
    is_odd = lax.rem(mb, 2)
    partner = mb + 1 - 2 * is_odd

    def direct(d, q):
        return pltpu.make_async_remote_copy(
            pout.at[q, d], pin.at[q, pair], s3.at[d, q], r3.at[pair, q],
            device_id=(d, me), device_id_type=MESH,
        )

    def relay(d, q):
        return pltpu.make_async_remote_copy(
            pout.at[q, d], pin.at[q, B // 2 + d], s3.at[d, q], r3.at[B // 2 + d, q],
            device_id=(partner, me), device_id_type=MESH,
        )

    def arrival(p, q):
        return pltpu.make_async_remote_copy(
            pout.at[q, mb], pin.at[q, p], s3.at[mb, q], r3.at[p, q],
            device_id=(partner, me), device_id_type=MESH,
        )

    def above(d):
        return jnp.where(lax.div(d, 2) > pair, 1, 0)

    def partial(d, g):
        return dot(x[...], wgu[lax.rem(d - mb + B, B), g])

    def far(i):
        return lax.rem(2 * pair + 2 + i, B)

    for k in range(B):
        for g in range(G):
            up_copy(0, k, g).wait()
            up_copy(1, k, g).wait()

    @pl.loop(0, G * (B - 2))
    def _(n):
        d, g = far(lax.rem(n, B - 2)), lax.div(n, B - 2)

        @pl.when(above(d) != is_odd)
        def _():
            pout[g, d] = partial(d, g).astype(BF)
            relay(d, g).start()

    @pl.loop(0, G)
    def _(g):
        pout[g, partner] = partial(partner, g).astype(BF)
        direct(partner, g).start()

    @pl.loop(0, G)
    def _(g):
        pout[g, mb] = partial(mb, g).astype(BF)

    @pl.loop(0, G * (B - 2))
    def _(n):
        d, g = far(lax.rem(n, B - 2)), lax.div(n, B - 2)

        @pl.when(above(d) == is_odd)
        def _():
            own = partial(d, g)
            arrival(B // 2 + d, g).wait_recv()
            pout[g, d] = (own + pin[g, B // 2 + d].astype(F32)).astype(BF)
            direct(d, g).start()

    def send4(k, g):
        cols = slice(g * FH, (g + 1) * FH)
        return pltpu.make_async_remote_copy(
            hin.at[0, :, cols], hin.at[k, :, cols], s4.at[k, g], r4.at[k, g],
            device_id=(bulk_at(k), me), device_id_type=MESH,
        )

    for g in range(G):
        total = pout[g, mb].astype(F32)
        for p in range(B // 2):
            arrival(p, g).wait_recv()
            total = total + pin[g, p].astype(F32)
        gate = total[:, :FH]
        hin[0, :, g * FH : (g + 1) * FH] = (
            gate / (1.0 + jnp.exp(-gate)) * total[:, FH:]
        ).astype(BF)
        for k in far_first:
            send4(k, g).start()
    for k in range(B):
        down_copy(k).wait()
    acc[...] = dot(hin[0], wd[0])
    for k in range(1, B - 1):
        for g in range(G):
            send4(k, g).wait_recv()
        acc[...] += dot(hin[k], wd[k])

    rr = xs

    def send5(k, h, at):
        return pltpu.make_async_remote_copy(
            rr.at[h, block(k)], back.at[h, block(at)], s5.at[k, h], r5.at[k, h],
            device_id=(mb, expert_at(-k)), device_id_type=MESH,
        )

    for g in range(G):
        send4(B - 1, g).wait_recv()
    for h in range(H):
        for k in range(1, E):
            send2(k, h).wait_send()
        cols = slice(h * DH, (h + 1) * DH)
        rows = acc[:, cols] + dot(hin[B - 1], wd[B - 1, :, cols])
        rr[h] = dot(p2t[...], rows.astype(BF)).astype(BF)
        for k in range(1, E):
            send5(k, h, me).start()
        back[h, block(me)] = rr[h, 0:RP]

    def send6(k, h, at):
        return pltpu.make_async_remote_copy(
            rb.at[k, h], fin.at[at, h], s6.at[k, h], r6.at[k, h],
            device_id=(bulk_at(k), me), device_id_type=MESH,
        )

    def keep(h):
        return pltpu.make_async_copy(rb.at[0, h], fin.at[mb, h], fsem.at[h])

    for h in range(H):
        for k in range(1, E):
            send5(k, h, expert_at(k)).wait_recv()
        for k in order:
            rb[k, h] = dot(p1t[bulk_at(k)], back[h]).astype(BF)
            if k:
                send6(k, h, mb).start()
            else:
                keep(h).start()
    for copy in side:
        copy.wait()
    for k in range(1, B):
        for h in range(H):
            send1(k, h).wait_send()
            send6(k, h, mb).wait_send()
        for q in range(G):
            direct(bulk_at(k), q).wait_send()
            send4(k, q).wait_send()
    for k in range(1, E):
        for h in range(H):
            send5(k, h, me).wait_send()
    for h in range(H):
        keep(h).wait()
        for k in range(1, B):
            send6(k, h, bulk_at(-k)).wait_recv()


def combine_kernel(fin, cs, ld, out_hbm, load, out, sems):
    B, H, SL, DH = fin.shape
    load[...] = ld[:1].astype(jnp.int32)
    copies = []
    for b in range(B):
        for h in range(H):
            rows = fin[b, h]
            at = (b * H + h) * DH
            out[:, at : at + DH] = (
                dot(cs[0], rows) + (dot(cs[1], rows) + dot(cs[2], rows))
            ).astype(BF)
        cols = pl.ds(b * H * DH, H * DH)
        copies.append(pltpu.make_async_copy(out.at[:, cols], out_hbm.at[:, cols], sems.at[b]))
        copies[-1].start()
    for copy in copies:
        copy.wait()


def on_device(tokens, expert_ids, gate_values, placement, gate_weight, up_weight, down_weight):
    E = lax.axis_size("expert")
    B = lax.axis_size("bulk")
    T, D = tokens.shape
    DS = gate_weight.shape[1]
    FB = gate_weight.shape[2] // B
    SL = E * CAP
    RQ = B * CAP
    RP = -(-RQ // 16) * 16
    R = E * RQ
    p1 = np.zeros((B, E * RP, SL), np.float32)
    p2 = np.zeros((R, E * RP), np.float32)
    for e in range(E):
        for q in range(RQ):
            p1[q // CAP, e * RP + q, e * CAP + q % CAP] = 1.0
            p2[e * RQ + q, e * RP + q] = 1.0
    p1t = np.swapaxes(p1, 1, 2)
    consts = [jnp.asarray(a.astype(ml_dtypes.bfloat16)) for a in (p1, p1t, p2, p2.T)]
    H = 2 if DS % 256 == 0 else 1
    G = FB // 128 if FB % 128 == 0 else 1
    DH = DS // H
    FH = FB // G
    vmem = pl.BlockSpec(memory_space=pltpu.VMEM)
    hbm = pl.BlockSpec(memory_space=pl.ANY)
    dma = pltpu.SemaphoreType.DMA
    buffers = [
        (T, D), (B, G, DS, 2 * FH), (B, FB, DS),
        (B, H, SL, DH), (B, H, SL, DH), (H, E * RP, DH), (H, E * RP, DH), (R, DS),
        (G, B, R, 2 * FH), (G, B + B // 2, R, 2 * FH), (B, R, FB), (R, DS),
        (H, E * RP, DH), (B, H, SL, DH), (3, T, SL), (8, E),
    ]
    sems = [(B, H), (B, H), (E, H), (E, H)] + [(B, G), (B + B // 2, G), (B, G), (B, G)] + [(E, H), (E, H), (B, H), (B, H)]
    fin, cs, ld = pl.pallas_call(
        functools.partial(kernel, B, E, RP, H, G),
        out_shape=(
            jax.ShapeDtypeStruct((B, H, SL, DH), BF),
            jax.ShapeDtypeStruct((3, T, SL), BF),
            jax.ShapeDtypeStruct((8, E), F32),
        ),
        in_specs=[hbm] + [vmem] * 7 + [hbm] * 3,
        out_specs=(hbm, hbm, hbm),
        scratch_shapes=[pltpu.VMEM(d, F32 if i in (11, 15) else BF) for i, d in enumerate(buffers)]
        + [dma, dma((2,)), dma((H,)), dma((2, B, G)), dma((B,))]
        + [dma(n) for n in sems],
        compiler_params=pltpu.CompilerParams(
            collective_id=0, has_side_effects=True, vmem_limit_bytes=62 * 1024 * 1024
        ),
    )(tokens, expert_ids.T, gate_values.T, placement.reshape(1, E), *consts,
      gate_weight, up_weight, down_weight)
    return pl.pallas_call(
        combine_kernel,
        out_shape=(
            jax.ShapeDtypeStruct((T, D), BF),
            jax.ShapeDtypeStruct((1, E), jnp.int32),
        ),
        in_specs=[vmem] * 3,
        out_specs=(hbm, vmem),
        scratch_shapes=[pltpu.VMEM((T, D), BF), dma((B,))],
    )(fin, cs, ld)


def solution(mesh):
    placed = (
        P(("bulk", "expert"), None),
        P(("bulk", "expert"), None),
        P(("bulk", "expert"), None),
        P(),
        P("expert", "bulk", None),
        P("expert", "bulk", None),
        P("expert", None, "bulk"),
    )
    return jax.shard_map(
        on_device,
        mesh=mesh,
        in_specs=placed,
        out_specs=(P(("bulk", "expert"), None), P(("bulk", "expert"), None)),
        check_vma=False,
    )
```

```python
import functools

import jax
import jax.numpy as jnp
import ml_dtypes
import numpy as np
from jax import lax
from jax.experimental import pallas as pl
from jax.experimental.pallas import tpu as pltpu
from jax.sharding import PartitionSpec as P

CAP = 3
BF = jnp.bfloat16
F32 = jnp.float32
MESH = pl.DeviceIdType.MESH


def dot(a, b):
    return jnp.dot(a, b, preferred_element_type=F32)


def across(a, b):
    return lax.dot_general(a, b, (((1,), (1,)), ((), ())), preferred_element_type=F32)


def kernel(
    B, E, G, tok_hbm, ids, gv, place, spread, unpack, pack, wg_hbm, wu_hbm, wd_hbm,
    out_hbm, load, tok, sel, og, xr, x, wgu, wd, pout, pin, prel, hin, acc, rr, fin, comb, outv,
    tsem, wsem, dsem, osem, s1, r1, s2, r2, s3, r3, s4, r4, s5, r5,
):
    TOP, T = ids.shape
    SL = E * CAP
    DS = wg_hbm.shape[1]
    FB = wg_hbm.shape[2] // B
    FH = FB // G
    NJ = DS // 128
    MR = spread.shape[0] // E
    EM = E * MR
    PAIRS = B // 2
    RG = 2 * SL
    DC = DS // 2 if DS % 256 == 0 else 128
    mb = lax.axis_index("bulk")
    me = lax.axis_index("expert")
    pair = lax.div(mb, 2)
    is_odd = lax.rem(mb, 2)
    partner = mb + 1 - 2 * is_odd

    def expert_at(k):
        return lax.rem(me + k, E)

    def group_at(n):
        return lax.rem(pair + n, PAIRS)

    def far(i):
        return lax.rem(2 * pair + 2 + i, B)

    def above(d):
        return jnp.where(lax.div(d, 2) > pair, 1, 0)

    def ahead(d):
        return above(d) == is_odd

    inner = jnp.where(is_odd == 1, pair < PAIRS - 1, pair > 0)
    outer = jnp.logical_not(inner)

    tok_copy = pltpu.make_async_copy(tok_hbm, tok, tsem)
    tok_copy.start()
    barrier = pltpu.get_barrier_semaphore()

    @pl.loop(1, B * E)
    def _(n):
        other = (lax.rem(mb + lax.div(n, E), B), lax.rem(me + lax.rem(n, E), E))
        pl.semaphore_signal(barrier, inc=1, device_id=other, device_id_type=MESH)

    def up_copy(i, d, g):
        cols = pl.ds(pl.multiple_of(d * FB + g * FH, FH), FH)
        return pltpu.make_async_copy(
            (wg_hbm, wu_hbm)[i].at[0, :, cols],
            wgu.at[d, g, :, i * FH : (i + 1) * FH],
            wsem.at[i, d, g],
        )

    def down_copy(k):
        rows = slice(k * FB, (k + 1) * FB)
        return pltpu.make_async_copy(wd_hbm.at[0, rows, :], wd.at[k], dsem.at[k])

    def fetch_far():
        @pl.loop(0, G * (B - 2))
        def _(n):
            for i in range(2):
                up_copy(i, far(lax.rem(n, B - 2)), lax.div(n, B - 2)).start()

    pl.when(outer)(fetch_far)

    @pl.loop(0, 2 * G)
    def _(n):
        d = jnp.where(n < G, partner, mb)
        for i in range(2):
            up_copy(i, d, lax.rem(n, G)).start()

    pl.when(inner)(fetch_far)
    for k in range(B):
        down_copy(k).start()

    slot = lax.broadcasted_iota(jnp.int32, (SL, T), 0)
    slot_expert = lax.div(slot, CAP)
    slot_rank = slot - slot_expert * CAP
    named = jnp.zeros((SL, T), F32)
    gates = jnp.zeros((SL, T), F32)
    for j in range(TOP):
        hit = ids[j : j + 1, :] == slot_expert
        named = named + jnp.where(hit, 1.0, 0.0)
        gates = gates + jnp.where(hit, gv[j : j + 1, :], 0.0)
    t_row = lax.broadcasted_iota(jnp.int32, (T, T), 0)
    t_col = lax.broadcasted_iota(jnp.int32, (T, T), 1)
    before = jnp.where(t_row < t_col, 1.0, 0.0).astype(BF)
    rank = dot(named.astype(BF), before)
    chosen = jnp.where(rank == slot_rank.astype(F32), named, 0.0)

    many = 128 // T
    KJ = sel.shape[1] // T
    wide = dot(spread[...], jnp.concatenate([chosen] * many, axis=1).astype(BF))
    row = lax.broadcasted_iota(jnp.int32, (EM, 128), 0)
    lane = lax.broadcasted_iota(jnp.int32, (EM, 128), 1)
    tile = lax.div(lax.rem(row, MR), CAP) - lax.div(lane, T)
    for i in range(KJ // many):
        sel[:, i * 128 : (i + 1) * 128] = jnp.where(tile == i * many, wide, 0.0).astype(BF)

    def send1(b, e):
        return pltpu.make_async_remote_copy(
            og.at[b, e], xr.at[mb, me], s1.at[b], r1.at[pair],
            device_id=(b, e), device_id_type=MESH,
        )

    def fill(q):
        stack = []
        for j in range(NJ):
            cols = [pl.ds(pl.multiple_of((2 * q + i) * DS + j * 128, 128), 128) for i in range(2)]
            stack.append(jnp.concatenate([tok[:, c] for c in cols], axis=1))
        for j in range(NJ, KJ):
            stack.append(jnp.zeros((T, 256), BF))
        rows = dot(sel[...], jnp.concatenate(stack, axis=0)).astype(BF)
        og[2 * q] = rows[:, :128].reshape(E, MR, 128)
        og[2 * q + 1] = rows[:, 128:].reshape(E, MR, 128)

    tok_copy.wait()
    fill(pair)
    pl.semaphore_wait(barrier, B * E - 1)
    mine = pltpu.make_async_copy(og.at[mb, me], xr.at[mb, me], r1.at[pair])
    mine.start()

    @pl.loop(0, E)
    def _(k):
        send1(partner, expert_at(k)).start()

    @pl.loop(1, E)
    def _(k):
        send1(mb, expert_at(k)).start()

    for n in range(1, PAIRS):
        q = group_at(n)
        fill(q)

        @pl.loop(0, E)
        def _(k):
            send1(2 * q, expert_at(k)).start()
            send1(2 * q + 1, expert_at(k)).start()

    member = jnp.zeros((E, T), F32)
    e_iota = lax.broadcasted_iota(jnp.int32, (E, T), 0)
    for j in range(TOP):
        member = member + jnp.where(ids[j : j + 1, :] == e_iota, 1.0, 0.0)
    odd_t = lax.rem(lax.broadcasted_iota(jnp.int32, (8, T), 1), 2) == 1
    odd = jnp.where(odd_t, 1.0, 0.0).astype(BF)
    even = jnp.where(odd_t, 0.0, 1.0).astype(BF)
    er = lax.broadcasted_iota(jnp.int32, (E, E), 0)
    ec = lax.broadcasted_iota(jnp.int32, (E, E), 1)
    shift = jnp.where(er == lax.rem(ec + 1, E), 1.0, 0.0).astype(BF)
    home = jnp.where(er == place[...], 1.0, 0.0).astype(BF)
    member = member.astype(BF)
    loads = across(across(odd, member).astype(BF), shift) + across(
        across(even, member).astype(BF), home
    )
    load[...] = loads[:1].astype(jnp.int32)
    eye = jnp.where(t_row == t_col, 1.0, 0.0).astype(BF)
    weigh = across(eye, (chosen * gates).astype(BF)).astype(BF)
    weigh = across(weigh, spread[...])
    col_tile = lax.div(lax.rem(lax.broadcasted_iota(jnp.int32, (T, EM), 1), MR), CAP)
    for j in range(NJ):
        comb[j * T : (j + 1) * T, :] = jnp.where(col_tile == j, weigh, 0.0).astype(BF)

    def both(ref, q):
        return jnp.concatenate(
            [ref[2 * q].reshape(EM, 128), ref[2 * q + 1].reshape(EM, 128)], axis=1
        )

    def gather(q):
        whole = xr.at[pl.ds(2 * q, 2)]
        pltpu.make_async_copy(whole, whole, r1.at[q]).wait()
        rows = dot(unpack[...], both(xr, q))
        for j in range(NJ):
            part = rows[j * SL : (j + 1) * SL]
            x[q, :, j * 128 : (j + 1) * 128] = jnp.concatenate(
                [part[:, :128], part[:, 128:]], axis=0
            ).astype(BF)

    def partial(q, d, g, first):
        if first:
            up_copy(0, d, g).wait()
            up_copy(1, d, g).wait()
        return dot(x[q], wgu[d, g])

    def relay(d, g, q):
        return pltpu.make_async_remote_copy(
            pout.at[g, d, q], prel.at[g, d, q], s2.at[g, d, q], r2.at[g, d, q],
            device_id=(partner, me), device_id_type=MESH,
        )

    def summed(d, g, q, at):
        return pltpu.make_async_remote_copy(
            pout.at[g, d, q], pin.at[g, at, q], s2.at[g, d, q], r3.at[g, at, q],
            device_id=(d, me), device_id_type=MESH,
        )

    def direct(g):
        return pltpu.make_async_remote_copy(
            pout.at[g, partner], pin.at[g, pair], s3.at[g], r3.at[g, pair, 0],
            device_id=(partner, me), device_id_type=MESH,
        )

    for n in range(PAIRS):
        q = group_at(n)
        gather(q)

        @pl.loop(0, G * (B - 2))
        def _(m):
            d, g = far(lax.rem(m, B - 2)), lax.div(m, B - 2)

            @pl.when(jnp.logical_not(ahead(d)))
            def _():
                pout[g, d, q] = partial(q, d, g, n == 0).astype(BF)
                relay(d, g, q).start()

        @pl.loop(0, G)
        def _(g):
            pout[g, partner, q] = partial(q, partner, g, n == 0).astype(BF)
            if n == PAIRS - 1:
                direct(g).start()

        @pl.loop(0, G)
        def _(g):
            pout[g, mb, q] = partial(q, mb, g, n == 0).astype(BF)

        @pl.loop(0, G * (B - 2))
        def _(m):
            d, g = far(lax.rem(m, B - 2)), lax.div(m, B - 2)

            @pl.when(ahead(d))
            def _():
                own = partial(q, d, g, n == 0)
                relay(d, g, q).wait_recv()
                pout[g, d, q] = (own + prel[g, d, q].astype(F32)).astype(BF)
                summed(d, g, q, pair).start()

    def share(s, d, g):
        cols = slice(g * FH, (g + 1) * FH)
        return pltpu.make_async_remote_copy(
            hin.at[s, :, cols], hin.at[s, :, cols], s4.at[s, d, g], r4.at[s, g],
            device_id=(d, me), device_id_type=MESH,
        )

    def near(d):
        return ahead(d) & (lax.rem(d, 2) != is_odd)

    def opposite(d):
        return ahead(d) & (lax.rem(d, 2) == is_odd)

    def pass_on(g):
        @pl.when(inner)
        def _():
            share(partner, mb, g).wait_recv()
            for i in range(B - 2):

                @pl.when(near(far(i)))
                def _():
                    share(partner, far(i), g).start()

    def hand_over(g):
        for i in range(B - 2):

            @pl.when(opposite(far(i)))
            def _():
                share(far(i), mb, g).wait_recv()
                share(far(i), partner, g).start()

    for g in range(G):
        direct(g).wait_recv()
        total = pout[g, mb].astype(F32) + pin[g, pair].astype(F32)
        for n in range(1, PAIRS):
            p = group_at(n)
            for q in range(PAIRS):
                summed(mb, g, q, p).wait_recv()
            total = total + pin[g, p].astype(F32)
        total = total.reshape(PAIRS * RG, 2 * FH)
        gate = total[:, :FH]
        hin[mb, :, g * FH : (g + 1) * FH] = (
            gate / (1.0 + jnp.exp(-gate)) * total[:, FH:]
        ).astype(BF)
        share(mb, partner, g).start()
        for i in range(B - 2):

            @pl.when(ahead(far(i)))
            def _():
                share(mb, far(i), g).start()

    for g in range(G):
        pass_on(g)
        if g:
            hand_over(g - 1)
    hand_over(G - 1)

    def add_down(s, first):
        for c in range(DS // DC):
            cols = slice(c * DC, (c + 1) * DC)
            part = dot(hin[s], wd[s, :, cols]).reshape(PAIRS, RG, DC)
            if first:
                acc[:, :, cols] = part
            else:
                acc[:, :, cols] += part

    for k in range(B):
        down_copy(k).wait()
    add_down(mb, True)

    def source(j):
        after = jnp.where(inner, j - 1, j)
        turn = jnp.where(lax.rem(pair, 2) == 1, after, B - 3 - after)
        return jnp.where(jnp.where(inner, j == 0, j == B - 2), partner, far(turn))

    @pl.loop(0, B - 1)
    def _(j):
        s = source(j)

        @pl.when(jnp.logical_not(jnp.where(s == partner, inner, opposite(s))))
        def _():
            for g in range(G):
                share(s, mb, g).wait_recv()

        add_down(s, False)

    def send5(b, e):
        return pltpu.make_async_remote_copy(
            rr.at[b, e], fin.at[mb, me], s5.at[b], r5.at[pair],
            device_id=(b, e), device_id_type=MESH,
        )

    for n in range(PAIRS):
        q = group_at(n)
        stack = []
        for j in range(NJ):
            cols = slice(j * 128, (j + 1) * 128)
            stack.append(jnp.concatenate([acc[q, :SL, cols], acc[q, SL:, cols]], axis=1))
        rows = dot(pack[...], jnp.concatenate(stack, axis=0).astype(BF)).astype(BF)
        rr[2 * q] = rows[:, :128].reshape(E, MR, 128)
        rr[2 * q + 1] = rows[:, 128:].reshape(E, MR, 128)
        if n == 0:
            home_copy = pltpu.make_async_copy(rr.at[mb, me], fin.at[mb, me], r5.at[pair])
            home_copy.start()

            @pl.loop(0, E)
            def _(k):
                send5(partner, expert_at(k)).start()

            @pl.loop(1, E)
            def _(k):
                send5(mb, expert_at(k)).start()
        else:

            @pl.loop(0, E)
            def _(k):
                send5(2 * q, expert_at(k)).start()
                send5(2 * q + 1, expert_at(k)).start()

    def keep(q):
        cols = pl.ds(pl.multiple_of(2 * q * DS, 128), 2 * DS)
        return pltpu.make_async_copy(outv.at[:, cols], out_hbm.at[:, cols], osem.at[q])

    for n in range(PAIRS):
        q = group_at(n)
        whole = fin.at[pl.ds(2 * q, 2)]
        pltpu.make_async_copy(whole, whole, r5.at[q]).wait()
        rows = dot(comb[...], both(fin, q)).astype(BF)
        for j in range(NJ):
            for i in range(2):
                cols = pl.ds(pl.multiple_of((2 * q + i) * DS + j * 128, 128), 128)
                outv[:, cols] = rows[j * T : (j + 1) * T, i * 128 : (i + 1) * 128]
        keep(q).start()

    for buf, sem in ((og, s1), (rr, s5)):
        for k in range(1, B):
            whole = buf.at[lax.rem(mb + k, B)]
            pltpu.make_async_copy(whole, whole, sem.at[lax.rem(mb + k, B)]).wait()
        rest = buf.at[mb, pl.ds(0, E - 1)]
        pltpu.make_async_copy(rest, rest, sem.at[mb]).wait()
    for g in range(G):
        direct(g).wait_send()
        share(mb, partner, g).wait_send()
        for i in range(B - 2):
            for q in range(PAIRS):
                relay(far(i), g, q).wait_send()

            @pl.when(ahead(far(i)))
            def _():
                share(mb, far(i), g).wait_send()

            @pl.when(near(far(i)))
            def _():
                share(partner, far(i), g).wait_send()

            @pl.when(opposite(far(i)))
            def _():
                share(far(i), partner, g).wait_send()

    for q in range(PAIRS):
        keep(q).wait()


def on_device(tokens, expert_ids, gate_values, placement, gate_weight, up_weight, down_weight):
    E = lax.axis_size("expert")
    B = lax.axis_size("bulk")
    T, D = tokens.shape
    TOP = expert_ids.shape[1]
    DS = gate_weight.shape[1]
    FB = gate_weight.shape[2] // B
    SL = E * CAP
    NJ = DS // 128
    MR = -(-NJ * CAP // 16) * 16
    EM = E * MR
    PAIRS = B // 2
    RG = 2 * SL
    G = FB // 128
    FH = FB // G
    KJ = -(-NJ * T // 128) * 128 // T
    spread = np.zeros((EM, SL), np.float32)
    pack = np.zeros((EM, NJ * SL), np.float32)
    for e in range(E):
        for j in range(NJ):
            for c in range(CAP):
                spread[e * MR + j * CAP + c, e * CAP + c] = 1.0
                pack[e * MR + j * CAP + c, j * SL + e * CAP + c] = 1.0
    consts = [jnp.asarray(a.astype(ml_dtypes.bfloat16)) for a in (spread, pack.T, pack)]
    vmem = pl.BlockSpec(memory_space=pltpu.VMEM)
    hbm = pl.BlockSpec(memory_space=pl.ANY)
    dma = pltpu.SemaphoreType.DMA
    buffers = [
        ((T, D), BF), ((EM, KJ * T), BF), ((B, E, MR, 128), BF), ((B, E, MR, 128), BF),
        ((PAIRS, RG, DS), BF), ((B, G, DS, 2 * FH), BF), ((B, FB, DS), BF),
        ((G, B, PAIRS, RG, 2 * FH), BF), ((G, PAIRS, PAIRS, RG, 2 * FH), BF),
        ((G, B, PAIRS, RG, 2 * FH), BF), ((B, PAIRS * RG, FB), BF), ((PAIRS, RG, DS), F32),
        ((B, E, MR, 128), BF), ((B, E, MR, 128), BF), ((NJ * T, EM), BF), ((T, D), BF),
    ]
    sems = [
        (2, B, G), (B,), (PAIRS,), (B,), (PAIRS,), (G, B, PAIRS), (G, B, PAIRS),
        (G,), (G, PAIRS, PAIRS), (B, B, G), (B, G), (B,), (PAIRS,),
    ]
    return pl.pallas_call(
        functools.partial(kernel, B, E, G),
        out_shape=(
            jax.ShapeDtypeStruct((T, D), BF),
            jax.ShapeDtypeStruct((1, E), jnp.int32),
        ),
        in_specs=[hbm] + [vmem] * 6 + [hbm] * 3,
        out_specs=(hbm, vmem),
        scratch_shapes=[pltpu.VMEM(*b) for b in buffers] + [dma] + [dma(n) for n in sems],
        compiler_params=pltpu.CompilerParams(
            collective_id=0, has_side_effects=True, vmem_limit_bytes=62 * 1024 * 1024
        ),
    )(tokens, expert_ids.T, gate_values.T, placement.reshape(1, E), *consts,
      gate_weight, up_weight, down_weight)


def solution(mesh):
    placed = (
        P(("bulk", "expert"), None),
        P(("bulk", "expert"), None),
        P(("bulk", "expert"), None),
        P(),
        P("expert", "bulk", None),
        P("expert", "bulk", None),
        P("expert", None, "bulk"),
    )
    return jax.shard_map(
        on_device,
        mesh=mesh,
        in_specs=placed,
        out_specs=(P(("bulk", "expert"), None), P(("bulk", "expert"), None)),
        check_vma=False,
    )
```

```python
import functools

import jax
import jax.numpy as jnp
import ml_dtypes
import numpy as np
from jax import lax
from jax.experimental import pallas as pl
from jax.experimental.pallas import tpu as pltpu
from jax.sharding import PartitionSpec as P

CAP = 3
BF = jnp.bfloat16
F32 = jnp.float32
MESH = pl.DeviceIdType.MESH


def dot(a, b):
    return jnp.dot(a, b, preferred_element_type=F32)


def across(a, b):
    return lax.dot_general(a, b, (((1,), (1,)), ((), ())), preferred_element_type=F32)


def kernel(
    B, E, G, tok_hbm, ids_hbm, gv_hbm, spread_hbm, tile_hbm, unpack_hbm, turn_hbm, pack_hbm,
    wg_hbm, wu_hbm, wd_hbm, fin, comb_hbm,
    tok, ids, gv, spread, tile, unpack, turn, pack,
    sel, og, xr, x, wgu, wd, pout, pin, prel, hin, acc, rr, comb,
    isem, wsem, dsem, osem, s1, r1, s2, r2, s3, r3, s4, r4, s5, r5,
):
    TOP, T = ids.shape
    SL = E * CAP
    DS = wg_hbm.shape[1]
    FB = wg_hbm.shape[2] // B
    FH = FB // G
    NJ = DS // 128
    MR = spread.shape[0] // E
    EM = E * MR
    PAIRS = B // 2
    RG = 2 * SL
    DC = DS // 2 if DS % 256 == 0 else 128
    mb = lax.axis_index("bulk")
    me = lax.axis_index("expert")
    pair = lax.div(mb, 2)
    is_odd = lax.rem(mb, 2)
    partner = mb + 1 - 2 * is_odd

    def wrap(i, n):
        return jnp.where(i >= n, i - n, i)

    def expert_at(k):
        return wrap(me + k, E)

    def group_at(n):
        return wrap(pair + n, PAIRS)

    def far(i):
        return wrap(2 * pair + 2 + i, B)

    def above(d):
        return jnp.where(lax.div(d, 2) > pair, 1, 0)

    def ahead(d):
        return above(d) == is_odd

    inner = jnp.where(is_odd == 1, pair < PAIRS - 1, pair > 0)
    outer = jnp.logical_not(inner)

    pairs = (
        (ids_hbm, ids), (gv_hbm, gv), (spread_hbm, spread), (tile_hbm, tile), (tok_hbm, tok),
        (unpack_hbm, unpack), (turn_hbm, turn), (pack_hbm, pack),
    )
    inputs = [pltpu.make_async_copy(a, b, isem.at[i]) for i, (a, b) in enumerate(pairs)]
    barrier = pltpu.get_barrier_semaphore()
    for k in range(B):

        @pl.loop(0 if k else 1, E)
        def _(n):
            other = (wrap(mb + k, B), expert_at(n))
            pl.semaphore_signal(barrier, inc=1, device_id=other, device_id_type=MESH)

    for copy in inputs:
        copy.start()

    def up_copy(i, d, g):
        cols = pl.ds(pl.multiple_of(d * FB + g * FH, FH), FH)
        return pltpu.make_async_copy(
            (wg_hbm, wu_hbm)[i].at[0, :, cols],
            wgu.at[d, g, :, i * FH : (i + 1) * FH],
            wsem.at[i, d, g],
        )

    def down_copy(k):
        rows = slice(k * FB, (k + 1) * FB)
        return pltpu.make_async_copy(wd_hbm.at[0, rows, :], wd.at[k], dsem.at[k])

    def fetch_far():
        @pl.loop(0, G)
        def _(g):
            @pl.loop(0, B - 2)
            def _(n):
                for i in range(2):
                    up_copy(i, far(n), g).start()

    pl.when(outer)(fetch_far)

    for d in (partner, mb):

        @pl.loop(0, G)
        def _(g):
            for i in range(2):
                up_copy(i, d, g).start()

    pl.when(inner)(fetch_far)
    for k in range(B):
        down_copy(k).start()

    for copy in inputs[:4]:
        copy.wait()
    slot = lax.broadcasted_iota(jnp.int32, (SL, T), 0)
    slot_expert = lax.div(slot, CAP)
    slot_rank = slot - slot_expert * CAP
    named = jnp.zeros((SL, T), F32)
    gates = jnp.zeros((SL, T), F32)
    for j in range(TOP):
        hit = ids[j : j + 1, :] == slot_expert
        named = named + jnp.where(hit, 1.0, 0.0)
        gates = gates + jnp.where(hit, gv[j : j + 1, :], 0.0)
    t_row = lax.broadcasted_iota(jnp.int32, (T, T), 0)
    t_col = lax.broadcasted_iota(jnp.int32, (T, T), 1)
    before = jnp.where(t_row < t_col, 1.0, 0.0).astype(BF)
    rank = dot(named.astype(BF), before)
    chosen = jnp.where(rank == slot_rank.astype(F32), named, 0.0)

    many = 128 // T
    KJ = sel.shape[1] // T
    wide = dot(spread[...], jnp.concatenate([chosen] * many, axis=1).astype(BF))
    row_tile = tile[...].astype(F32)
    for i in range(KJ // many):
        cols = slice(i * 128, (i + 1) * 128)
        sel[:, cols] = jnp.where(row_tile == i * many, wide, 0.0).astype(BF)

    def send1(b, e):
        return pltpu.make_async_remote_copy(
            og.at[b, e], xr.at[mb, me], s1.at[b], r1.at[pair],
            device_id=(b, e), device_id_type=MESH,
        )

    def fill(q):
        stack = []
        for j in range(NJ):
            cols = [pl.ds(pl.multiple_of((2 * q + i) * DS + j * 128, 128), 128) for i in range(2)]
            stack.append(jnp.concatenate([tok[:, c] for c in cols], axis=1))
        for j in range(NJ, KJ):
            stack.append(jnp.zeros((T, 256), BF))
        rows = dot(sel[...], jnp.concatenate(stack, axis=0)).astype(BF)
        og[2 * q] = rows[:, :128].reshape(E, MR, 128)
        og[2 * q + 1] = rows[:, 128:].reshape(E, MR, 128)

    def send_near(send):
        @pl.loop(0, E)
        def _(k):
            send(partner, expert_at(k)).start()

        @pl.loop(1, E)
        def _(k):
            send(mb, expert_at(k)).start()

    def send_far(send, q):
        @pl.loop(0, E)
        def _(k):
            send(2 * q, expert_at(k)).start()
            send(2 * q + 1, expert_at(k)).start()

    inputs[4].wait()
    fill(pair)
    pl.semaphore_wait(barrier, B * E - 1)
    pltpu.make_async_copy(og.at[mb, me], xr.at[mb, me], r1.at[pair]).start()
    send_near(send1)
    for n in range(1, PAIRS):
        fill(group_at(n))
        send_far(send1, group_at(n))

    eye = jnp.where(t_row == t_col, 1.0, 0.0).astype(BF)
    weigh = across(eye, (chosen * gates).astype(BF)).astype(BF)

    comb_copy = pltpu.make_async_copy(comb, comb_hbm, osem)

    def weigh_rows():
        wide = across(weigh, spread[...])
        col_tile = turn[...].astype(F32)
        for j in range(NJ):
            comb[j * T : (j + 1) * T, :] = jnp.where(col_tile == j, wide, 0.0).astype(BF)
        comb_copy.start()

    def both(ref, q):
        return jnp.concatenate(
            [ref[2 * q].reshape(EM, 128), ref[2 * q + 1].reshape(EM, 128)], axis=1
        )

    def gather(q):
        whole = xr.at[pl.ds(2 * q, 2)]
        pltpu.make_async_copy(whole, whole, r1.at[q]).wait()
        rows = dot(unpack[...], both(xr, q))
        for j in range(NJ):
            part = rows[j * SL : (j + 1) * SL]
            x[q, :, j * 128 : (j + 1) * 128] = jnp.concatenate(
                [part[:, :128], part[:, 128:]], axis=0
            ).astype(BF)

    def partial(q, d, g, first):
        if first:
            up_copy(0, d, g).wait()
            up_copy(1, d, g).wait()
        return dot(x[q], wgu[d, g])

    def relay(d, g, q):
        return pltpu.make_async_remote_copy(
            pout.at[g, d, q], prel.at[g, d, q], s2.at[g, d, q], r2.at[g, d, q],
            device_id=(partner, me), device_id_type=MESH,
        )

    def summed(d, g, q, at):
        return pltpu.make_async_remote_copy(
            pout.at[g, d, q], pin.at[g, at, q], s2.at[g, d, q], r3.at[g, at, q],
            device_id=(d, me), device_id_type=MESH,
        )

    def direct(g):
        return pltpu.make_async_remote_copy(
            pout.at[g, partner], pin.at[g, pair], s3.at[g], r3.at[g, pair, 0],
            device_id=(partner, me), device_id_type=MESH,
        )

    def each_far(body):
        @pl.loop(0, G)
        def _(g):
            @pl.loop(0, B - 2)
            def _(i):
                body(far(i), g)

    for copy in inputs[5:]:
        copy.wait()
    for n in range(PAIRS):
        q = group_at(n)
        first, last = n == 0, n == PAIRS - 1
        if last:
            weigh_rows()
        gather(q)

        def pass_half(d, g):
            pout[g, d, q] = partial(q, d, g, first).astype(BF)
            relay(d, g, q).start()

        def pass_sum(d, g):
            own = partial(q, d, g, first)
            relay(d, g, q).wait_recv()
            pout[g, d, q] = (own + prel[g, d, q].astype(F32)).astype(BF)
            summed(d, g, q, pair).start()

        each_far(lambda d, g: pl.when(jnp.logical_not(ahead(d)))(lambda: pass_half(d, g)))

        @pl.loop(0, G)
        def _(g):
            pout[g, partner, q] = partial(q, partner, g, first).astype(BF)
            if last:
                direct(g).start()

        @pl.loop(0, G)
        def _(g):
            pout[g, mb, q] = partial(q, mb, g, first).astype(BF)

        each_far(lambda d, g: pl.when(ahead(d))(lambda: pass_sum(d, g)))

    def share(s, d, g):
        cols = slice(g * FH, (g + 1) * FH)
        return pltpu.make_async_remote_copy(
            hin.at[s, :, cols], hin.at[s, :, cols], s4.at[s, d, g], r4.at[s, g],
            device_id=(d, me), device_id_type=MESH,
        )

    def opposite(d):
        return ahead(d) & (lax.rem(d, 2) == is_odd)

    def straight(d):
        return ahead(d) | (lax.rem(d, 2) != above(d))

    for g in range(G):
        direct(g).wait_recv()
        total = pout[g, mb].astype(F32) + pin[g, pair].astype(F32)
        for n in range(1, PAIRS):
            p = group_at(n)
            for q in range(PAIRS):
                summed(mb, g, q, p).wait_recv()
            total = total + pin[g, p].astype(F32)
        total = total.reshape(PAIRS * RG, 2 * FH)
        gate = total[:, :FH]
        hin[mb, :, g * FH : (g + 1) * FH] = (
            gate / (1.0 + jnp.exp(-gate)) * total[:, FH:]
        ).astype(BF)
        for i in range(B - 2):
            pl.when(straight(far(i)))(lambda: share(mb, far(i), g).start())
        share(mb, partner, g).start()

    def add_down(s, first):
        for c in range(DS // DC):
            cols = slice(c * DC, (c + 1) * DC)
            part = dot(hin[s], wd[s, :, cols]).reshape(PAIRS, RG, DC)
            if first:
                acc[:, :, cols] = part
            else:
                acc[:, :, cols] += part

    for k in range(B):
        down_copy(k).wait()
    add_down(mb, True)

    for g in range(G):
        for i in range(B - 2):

            @pl.when(opposite(far(i)))
            def _():
                share(far(i), mb, g).wait_recv()
                share(far(i), partner, g).start()

    @pl.loop(0, B - 1)
    def _(j):
        s = jnp.where(j == B - 2, partner, far(j))

        @pl.when((s == partner) | jnp.logical_not(opposite(s)))
        def _():
            for g in range(G):
                share(s, mb, g).wait_recv()

        add_down(s, False)

    def send5(b, e):
        return pltpu.make_async_remote_copy(
            rr.at[b, e], fin.at[mb, me], s5.at[b], r5.at[pair],
            device_id=(b, e), device_id_type=MESH,
        )

    for n in (*range(1, PAIRS), 0):
        q = group_at(n)
        stack = []
        for j in range(NJ):
            cols = slice(j * 128, (j + 1) * 128)
            stack.append(jnp.concatenate([acc[q, :SL, cols], acc[q, SL:, cols]], axis=1))
        rows = dot(pack[...], jnp.concatenate(stack, axis=0).astype(BF)).astype(BF)
        rr[2 * q] = rows[:, :128].reshape(E, MR, 128)
        rr[2 * q + 1] = rows[:, 128:].reshape(E, MR, 128)
        if n:
            send_far(send5, q)
        else:
            pltpu.make_async_copy(rr.at[mb, me], fin.at[mb, me], r5.at[pair]).start()
            send_near(send5)
    for q in range(PAIRS):
        whole = fin.at[pl.ds(2 * q, 2)]
        pltpu.make_async_copy(whole, whole, r5.at[q]).wait()

    for buf, sem in ((og, s1), (rr, s5)):
        for k in range(1, B):
            whole = buf.at[lax.rem(mb + k, B)]
            pltpu.make_async_copy(whole, whole, sem.at[lax.rem(mb + k, B)]).wait()
        rest = buf.at[mb, pl.ds(0, E - 1)]
        pltpu.make_async_copy(rest, rest, sem.at[mb]).wait()
    for g in range(G):
        direct(g).wait_send()
        share(mb, partner, g).wait_send()

        @pl.loop(0, B - 2)
        def _(i):
            d = far(i)
            pl.when(straight(d))(lambda: share(mb, d, g).wait_send())
            pl.when(opposite(d))(lambda: share(d, partner, g).wait_send())
            for q in range(PAIRS):
                relay(d, g, q).wait_send()

    comb_copy.wait()


def close_kernel(ids, place, fin_hbm, comb_hbm, out_hbm, load, fin, comb, out, isem, osem):
    T = ids.shape[1]
    E = place.shape[1]
    B, _, MR, _ = fin.shape
    EM = E * MR
    NJ = comb.shape[0] // T
    DS = NJ * 128
    comb_copy = pltpu.make_async_copy(comb_hbm, comb, isem.at[0])
    comb_copy.start()
    fetch = []
    for q in range(B // 2):
        two = pl.ds(2 * q, 2)
        fetch.append(pltpu.make_async_copy(fin_hbm.at[two], fin.at[two], isem.at[q + 1]))
        fetch[-1].start()
    member = jnp.zeros((E, T), F32)
    e_iota = lax.broadcasted_iota(jnp.int32, (E, T), 0)
    for j in range(ids.shape[0]):
        member = member + jnp.where(ids[j : j + 1, :] == e_iota, 1.0, 0.0)
    odd_t = lax.rem(lax.broadcasted_iota(jnp.int32, (8, T), 1), 2) == 1
    odd = jnp.where(odd_t, 1.0, 0.0).astype(BF)
    even = jnp.where(odd_t, 0.0, 1.0).astype(BF)
    er = lax.broadcasted_iota(jnp.int32, (E, E), 0)
    ec = lax.broadcasted_iota(jnp.int32, (E, E), 1)
    shift = jnp.where(er == lax.rem(ec + 1, E), 1.0, 0.0).astype(BF)
    home = jnp.where(er == place[...], 1.0, 0.0).astype(BF)
    member = member.astype(BF)
    loads = across(across(odd, member).astype(BF), shift) + across(
        across(even, member).astype(BF), home
    )
    load[...] = loads[:1].astype(jnp.int32)
    comb_copy.wait()
    store = []
    for q in range(B // 2):
        fetch[q].wait()
        both = [fin[2 * q + i].reshape(EM, 128) for i in range(2)]
        rows = dot(comb[...], jnp.concatenate(both, axis=1)).astype(BF)
        for i in range(2):
            for j in range(NJ):
                at = (2 * q + i) * DS + j * 128
                out[:, at : at + 128] = rows[j * T : (j + 1) * T, i * 128 : (i + 1) * 128]
        cols = slice(2 * q * DS, 2 * (q + 1) * DS)
        store.append(pltpu.make_async_copy(out.at[:, cols], out_hbm.at[:, cols], osem.at[q]))
        store[-1].start()
    for copy in store:
        copy.wait()


def on_device(tokens, expert_ids, gate_values, placement, gate_weight, up_weight, down_weight):
    E = lax.axis_size("expert")
    B = lax.axis_size("bulk")
    T, D = tokens.shape
    TOP = expert_ids.shape[1]
    DS = gate_weight.shape[1]
    FB = gate_weight.shape[2] // B
    SL = E * CAP
    NJ = DS // 128
    MR = -(-NJ * CAP // 16) * 16
    EM = E * MR
    PAIRS = B // 2
    RG = 2 * SL
    G = FB // 128
    FH = FB // G
    KJ = -(-NJ * T // 128) * 128 // T
    spread = np.zeros((EM, SL), np.float32)
    pack = np.zeros((EM, NJ * SL), np.float32)
    for e in range(E):
        for j in range(NJ):
            for c in range(CAP):
                spread[e * MR + j * CAP + c, e * CAP + c] = 1.0
                pack[e * MR + j * CAP + c, j * SL + e * CAP + c] = 1.0
    row_tile = np.arange(EM) % MR // CAP
    row_tile = np.where(row_tile < NJ, row_tile, 2 * KJ)
    tile = row_tile[:, None] - np.arange(128)[None, :] // T
    turn = np.broadcast_to(row_tile[None, :], (T, EM))
    tables = (spread, tile, pack.T, turn, pack)
    consts = [jnp.asarray(a.astype(ml_dtypes.bfloat16)) for a in tables]
    vmem = pl.BlockSpec(memory_space=pltpu.VMEM)
    hbm = pl.BlockSpec(memory_space=pl.ANY)
    dma = pltpu.SemaphoreType.DMA
    buffers = [
        ((T, D), BF), ((TOP, T), jnp.int32), ((TOP, T), F32),
        *((a.shape, BF) for a in tables),
        ((EM, KJ * T), BF), ((B, E, MR, 128), BF), ((B, E, MR, 128), BF),
        ((PAIRS, RG, DS), BF), ((B, G, DS, 2 * FH), BF), ((B, FB, DS), BF),
        ((G, B, PAIRS, RG, 2 * FH), BF), ((G, PAIRS, PAIRS, RG, 2 * FH), BF),
        ((G, B, PAIRS, RG, 2 * FH), BF), ((B, PAIRS * RG, FB), BF), ((PAIRS, RG, DS), F32),
        ((B, E, MR, 128), BF), ((NJ * T, EM), BF),
    ]
    sems = [
        (8,), (2, B, G), (B,), (), (B,), (PAIRS,), (G, B, PAIRS), (G, B, PAIRS),
        (G,), (G, PAIRS, PAIRS), (B, B, G), (B, G), (B,), (PAIRS,),
    ]
    named = expert_ids.T
    fin, comb = pl.pallas_call(
        functools.partial(kernel, B, E, G),
        out_shape=(
            jax.ShapeDtypeStruct((B, E, MR, 128), BF),
            jax.ShapeDtypeStruct((NJ * T, EM), BF),
        ),
        in_specs=[hbm] * 11,
        out_specs=(hbm, hbm),
        scratch_shapes=[pltpu.VMEM(*b) for b in buffers] + [dma(n) if n else dma for n in sems],
        compiler_params=pltpu.CompilerParams(
            collective_id=0, has_side_effects=True, vmem_limit_bytes=62 * 1024 * 1024
        ),
    )(tokens, named, gate_values.T, *consts, gate_weight, up_weight, down_weight)
    return pl.pallas_call(
        close_kernel,
        out_shape=(
            jax.ShapeDtypeStruct((T, D), BF),
            jax.ShapeDtypeStruct((1, E), jnp.int32),
        ),
        in_specs=[vmem, vmem, hbm, hbm],
        out_specs=(hbm, vmem),
        scratch_shapes=[
            pltpu.VMEM((B, E, MR, 128), BF), pltpu.VMEM((NJ * T, EM), BF), pltpu.VMEM((T, D), BF),
            dma((PAIRS + 1,)), dma((PAIRS,)),
        ],
    )(named, placement.reshape(1, E), fin, comb)


def solution(mesh):
    placed = (
        P(("bulk", "expert"), None),
        P(("bulk", "expert"), None),
        P(("bulk", "expert"), None),
        P(),
        P("expert", "bulk", None),
        P("expert", "bulk", None),
        P("expert", None, "bulk"),
    )
    return jax.shard_map(
        on_device,
        mesh=mesh,
        in_specs=placed,
        out_specs=(P(("bulk", "expert"), None), P(("bulk", "expert"), None)),
        check_vma=False,
    )
```

```python
import functools

import jax
import jax.numpy as jnp
import ml_dtypes
import numpy as np
from jax import lax
from jax.experimental import pallas as pl
from jax.experimental.pallas import tpu as pltpu
from jax.sharding import PartitionSpec as P

CAP = 3
BF = jnp.bfloat16
F32 = jnp.float32
MESH = pl.DeviceIdType.MESH


def dot(a, b):
    return jnp.dot(a, b, preferred_element_type=F32)


def across(a, b):
    return lax.dot_general(a, b, (((1,), (1,)), ((), ())), preferred_element_type=F32)


def kernel(
    B, E, G, tok_hbm, ids_hbm, gv_hbm, spread_hbm, tile_hbm, unpack_hbm, turn_hbm, pack_hbm,
    wg_hbm, wu_hbm, wd_hbm, fin, comb_hbm,
    tok, ids, gv, spread, tile, unpack, turn, pack,
    sel, og, xr, x, wgu, wd, pout, pin, prel, hin, acc, rr, comb,
    isem, wsem, dsem, osem, s1, r1, s2, r2, s3, r3, s4, r4, s5, r5,
):
    TOP, T = ids.shape
    SL = E * CAP
    DS = wg_hbm.shape[1]
    FB = wg_hbm.shape[2] // B
    FH = FB // G
    NJ = DS // 128
    MR = spread.shape[0] // E
    EM = E * MR
    PAIRS = B // 2
    RG = 2 * SL
    DC = DS // 2 if DS % 256 == 0 else 128
    mb = lax.axis_index("bulk")
    me = lax.axis_index("expert")
    pair = lax.div(mb, 2)
    is_odd = lax.rem(mb, 2)
    partner = mb + 1 - 2 * is_odd

    def wrap(i, n):
        return jnp.where(i >= n, i - n, i)

    def expert_at(k):
        return wrap(me + k, E)

    def group_at(n):
        return wrap(pair + n, PAIRS)

    def far(i):
        return wrap(2 * pair + 2 + i, B)

    def above(d):
        return jnp.where(lax.div(d, 2) > pair, 1, 0)

    def ahead(d):
        return above(d) == is_odd

    inner = jnp.where(is_odd == 1, pair < PAIRS - 1, pair > 0)
    outer = jnp.logical_not(inner)

    pairs = (
        (ids_hbm, ids), (gv_hbm, gv), (spread_hbm, spread), (tile_hbm, tile), (tok_hbm, tok),
        (unpack_hbm, unpack), (turn_hbm, turn), (pack_hbm, pack),
    )
    inputs = [pltpu.make_async_copy(a, b, isem.at[i]) for i, (a, b) in enumerate(pairs)]
    for copy in inputs[:5]:
        copy.start()
    barrier = pltpu.get_barrier_semaphore()
    for k in range(B):

        @pl.loop(0 if k else 1, E)
        def _(n):
            other = (wrap(mb + k, B), expert_at(n))
            pl.semaphore_signal(barrier, inc=1, device_id=other, device_id_type=MESH)

    for copy in inputs[5:]:
        copy.start()

    def up_copy(i, d, g):
        cols = pl.ds(pl.multiple_of(d * FB + g * FH, FH), FH)
        return pltpu.make_async_copy(
            (wg_hbm, wu_hbm)[i].at[0, :, cols],
            wgu.at[d, g, :, i * FH : (i + 1) * FH],
            wsem.at[i, d, g],
        )

    def down_copy(k):
        rows = slice(k * FB, (k + 1) * FB)
        return pltpu.make_async_copy(wd_hbm.at[0, rows, :], wd.at[k], dsem.at[k])

    def fetch_far():
        @pl.loop(0, G)
        def _(g):
            @pl.loop(0, B - 2)
            def _(n):
                for i in range(2):
                    up_copy(i, far(n), g).start()

    pl.when(outer)(fetch_far)

    for d in (partner, mb):

        @pl.loop(0, G)
        def _(g):
            for i in range(2):
                up_copy(i, d, g).start()

    pl.when(inner)(fetch_far)
    for k in range(B):
        down_copy(k).start()

    for copy in inputs[:4]:
        copy.wait()
    slot = lax.broadcasted_iota(jnp.int32, (SL, T), 0)
    slot_expert = lax.div(slot, CAP)
    slot_rank = slot - slot_expert * CAP
    named = jnp.zeros((SL, T), F32)
    gates = jnp.zeros((SL, T), F32)
    for j in range(TOP):
        hit = ids[j : j + 1, :] == slot_expert
        named = named + jnp.where(hit, 1.0, 0.0)
        gates = gates + jnp.where(hit, gv[j : j + 1, :], 0.0)
    t_row = lax.broadcasted_iota(jnp.int32, (T, T), 0)
    t_col = lax.broadcasted_iota(jnp.int32, (T, T), 1)
    before = jnp.where(t_row < t_col, 1.0, 0.0).astype(BF)
    rank = dot(named.astype(BF), before)
    chosen = jnp.where(rank == slot_rank.astype(F32), named, 0.0)

    many = 128 // T
    KJ = sel.shape[1] // T
    wide = dot(spread[...], jnp.concatenate([chosen] * many, axis=1).astype(BF))
    row_tile = tile[...].astype(F32)
    for i in range(KJ // many):
        cols = slice(i * 128, (i + 1) * 128)
        sel[:, cols] = jnp.where(row_tile == i * many, wide, 0.0).astype(BF)

    def send1(b, e):
        return pltpu.make_async_remote_copy(
            og.at[b, e], xr.at[mb, me], s1.at[b], r1.at[pair],
            device_id=(b, e), device_id_type=MESH,
        )

    def fill(q):
        stack = []
        for j in range(NJ):
            cols = [pl.ds(pl.multiple_of((2 * q + i) * DS + j * 128, 128), 128) for i in range(2)]
            stack.append(jnp.concatenate([tok[:, c] for c in cols], axis=1))
        for j in range(NJ, KJ):
            stack.append(jnp.zeros((T, 256), BF))
        rows = dot(sel[...], jnp.concatenate(stack, axis=0)).astype(BF)
        og[2 * q] = rows[:, :128].reshape(E, MR, 128)
        og[2 * q + 1] = rows[:, 128:].reshape(E, MR, 128)

    def send_near(send):
        @pl.loop(0, E)
        def _(k):
            send(partner, expert_at(k)).start()

        @pl.loop(1, E)
        def _(k):
            send(mb, expert_at(k)).start()

    def send_far(send, q):
        @pl.loop(0, E)
        def _(k):
            send(2 * q, expert_at(k)).start()
            send(2 * q + 1, expert_at(k)).start()

    inputs[4].wait()
    fill(pair)
    pl.semaphore_wait(barrier, B * E - 1)
    pltpu.make_async_copy(og.at[mb, me], xr.at[mb, me], r1.at[pair]).start()
    send_near(send1)
    for n in range(1, PAIRS):
        fill(group_at(n))
        send_far(send1, group_at(n))

    eye = jnp.where(t_row == t_col, 1.0, 0.0).astype(BF)
    weigh = across(eye, (chosen * gates).astype(BF)).astype(BF)

    comb_copy = pltpu.make_async_copy(comb, comb_hbm, osem)

    def weigh_rows():
        wide = across(weigh, spread[...])
        col_tile = turn[...].astype(F32)
        for j in range(NJ):
            comb[j * T : (j + 1) * T, :] = jnp.where(col_tile == j, wide, 0.0).astype(BF)
        comb_copy.start()

    def both(ref, q):
        return jnp.concatenate(
            [ref[2 * q].reshape(EM, 128), ref[2 * q + 1].reshape(EM, 128)], axis=1
        )

    def gather(q):
        whole = xr.at[pl.ds(2 * q, 2)]
        pltpu.make_async_copy(whole, whole, r1.at[q]).wait()
        rows = dot(unpack[...], both(xr, q))
        for j in range(NJ):
            part = rows[j * SL : (j + 1) * SL]
            x[q, :, j * 128 : (j + 1) * 128] = jnp.concatenate(
                [part[:, :128], part[:, 128:]], axis=0
            ).astype(BF)

    def partial(q, d, g, first):
        if first:
            up_copy(0, d, g).wait()
            up_copy(1, d, g).wait()
        return dot(x[q], wgu[d, g])

    def relay(d, g, q):
        return pltpu.make_async_remote_copy(
            pout.at[g, d, q], prel.at[g, d, q], s2.at[g, d, q], r2.at[g, d, q],
            device_id=(partner, me), device_id_type=MESH,
        )

    def summed(d, g, q, at):
        return pltpu.make_async_remote_copy(
            pout.at[g, d, q], pin.at[g, at, q], s2.at[g, d, q], r3.at[g, at, q],
            device_id=(d, me), device_id_type=MESH,
        )

    def direct(g):
        return pltpu.make_async_remote_copy(
            pout.at[g, partner], pin.at[g, pair], s3.at[g], r3.at[g, pair, 0],
            device_id=(partner, me), device_id_type=MESH,
        )

    def each_far(body):
        @pl.loop(0, G)
        def _(g):
            @pl.loop(0, B - 2)
            def _(i):
                body(far(i), g)

    for copy in inputs[5:]:
        copy.wait()
    for n in range(PAIRS):
        q = group_at(n)
        first, last = n == 0, n == PAIRS - 1
        if last:
            weigh_rows()
        gather(q)

        def pass_half(d, g):
            pout[g, d, q] = partial(q, d, g, first).astype(BF)
            relay(d, g, q).start()

        def pass_sum(d, g):
            own = partial(q, d, g, first)
            relay(d, g, q).wait_recv()
            pout[g, d, q] = (own + prel[g, d, q].astype(F32)).astype(BF)
            summed(d, g, q, pair).start()

        each_far(lambda d, g: pl.when(jnp.logical_not(ahead(d)))(lambda: pass_half(d, g)))

        @pl.loop(0, G)
        def _(g):
            pout[g, partner, q] = partial(q, partner, g, first).astype(BF)
            if last:
                direct(g).start()

        @pl.loop(0, G)
        def _(g):
            pout[g, mb, q] = partial(q, mb, g, first).astype(BF)

        each_far(lambda d, g: pl.when(ahead(d))(lambda: pass_sum(d, g)))

    def share(s, d, g):
        return pltpu.make_async_remote_copy(
            hin.at[s, g], hin.at[s, g], s4.at[s, d, g], r4.at[s, g],
            device_id=(d, me), device_id_type=MESH,
        )

    def opposite(d):
        return ahead(d) & (lax.rem(d, 2) == is_odd)

    def straight(d):
        return ahead(d) | (lax.rem(d, 2) != above(d))

    for g in range(G):
        direct(g).wait_recv()
        total = pout[g, mb].astype(F32) + pin[g, pair].astype(F32)
        for n in range(1, PAIRS):
            p = group_at(n)
            for q in range(PAIRS):
                summed(mb, g, q, p).wait_recv()
            total = total + pin[g, p].astype(F32)
        total = total.reshape(PAIRS * RG, 2 * FH)
        gate = total[:, :FH]
        hin[mb, g] = (
            gate / (1.0 + jnp.exp(-gate)) * total[:, FH:]
        ).astype(BF)
        for i in range(B - 2):
            pl.when(straight(far(i)))(lambda: share(mb, far(i), g).start())
        share(mb, partner, g).start()

    def add_down(s, first):
        hidden = jnp.concatenate([hin[s, g] for g in range(G)], axis=1)
        for c in range(DS // DC):
            cols = slice(c * DC, (c + 1) * DC)
            part = dot(hidden, wd[s, :, cols]).reshape(PAIRS, RG, DC)
            if first:
                acc[:, :, cols] = part
            else:
                acc[:, :, cols] += part

    for k in range(B):
        down_copy(k).wait()
    add_down(mb, True)

    for g in range(G):
        for i in range(B - 2):

            @pl.when(opposite(far(i)))
            def _():
                share(far(i), mb, g).wait_recv()
                share(far(i), partner, g).start()

    @pl.loop(0, B - 1)
    def _(j):
        turn = jnp.where(lax.rem(pair, 2) == 1, B - 2 - j, j - 1)
        s = jnp.where(j == 0, partner, far(turn))

        @pl.when((s == partner) | jnp.logical_not(opposite(s)))
        def _():
            for g in range(G):
                share(s, mb, g).wait_recv()

        add_down(s, False)

    def send5(b, e):
        return pltpu.make_async_remote_copy(
            rr.at[b, e], fin.at[mb, me], s5.at[b], r5.at[pair],
            device_id=(b, e), device_id_type=MESH,
        )

    for n in (*range(1, PAIRS), 0):
        q = group_at(n)
        stack = []
        for j in range(NJ):
            cols = slice(j * 128, (j + 1) * 128)
            stack.append(jnp.concatenate([acc[q, :SL, cols], acc[q, SL:, cols]], axis=1))
        rows = dot(pack[...], jnp.concatenate(stack, axis=0).astype(BF)).astype(BF)
        rr[2 * q] = rows[:, :128].reshape(E, MR, 128)
        rr[2 * q + 1] = rows[:, 128:].reshape(E, MR, 128)
        if n:
            send_far(send5, q)
        else:
            pltpu.make_async_copy(rr.at[mb, me], fin.at[mb, me], r5.at[pair]).start()
            send_near(send5)
    for q in range(PAIRS):
        whole = fin.at[pl.ds(2 * q, 2)]
        pltpu.make_async_copy(whole, whole, r5.at[q]).wait()

    for buf, sem in ((og, s1), (rr, s5)):
        for k in range(1, B):
            whole = buf.at[lax.rem(mb + k, B)]
            pltpu.make_async_copy(whole, whole, sem.at[lax.rem(mb + k, B)]).wait()
        rest = buf.at[mb, pl.ds(0, E - 1)]
        pltpu.make_async_copy(rest, rest, sem.at[mb]).wait()
    for g in range(G):
        direct(g).wait_send()
        share(mb, partner, g).wait_send()

        @pl.loop(0, B - 2)
        def _(i):
            d = far(i)
            pl.when(straight(d))(lambda: share(mb, d, g).wait_send())
            pl.when(opposite(d))(lambda: share(d, partner, g).wait_send())
            for q in range(PAIRS):
                relay(d, g, q).wait_send()

    comb_copy.wait()


def close_kernel(
    ids_hbm, place_hbm, fin_hbm, comb_hbm, out_hbm, load,
    ids, place, fin, comb, out, isem, nsem, osem,
):
    T = ids.shape[1]
    E = place.shape[1]
    B, _, MR, _ = fin.shape
    EM = E * MR
    NJ = comb.shape[0] // T
    DS = NJ * 128
    comb_copy = pltpu.make_async_copy(comb_hbm, comb, isem.at[0])
    comb_copy.start()
    fetch = []
    for q in range(B // 2):
        two = pl.ds(2 * q, 2)
        fetch.append(pltpu.make_async_copy(fin_hbm.at[two], fin.at[two], isem.at[q + 1]))
        fetch[-1].start()
    small = (
        pltpu.make_async_copy(ids_hbm, ids, nsem.at[0]),
        pltpu.make_async_copy(place_hbm, place, nsem.at[1]),
    )
    for copy in small:
        copy.start()
    for copy in small:
        copy.wait()
    member = jnp.zeros((E, T), F32)
    e_iota = lax.broadcasted_iota(jnp.int32, (E, T), 0)
    for j in range(ids.shape[0]):
        member = member + jnp.where(ids[j : j + 1, :] == e_iota, 1.0, 0.0)
    odd_t = lax.rem(lax.broadcasted_iota(jnp.int32, (8, T), 1), 2) == 1
    odd = jnp.where(odd_t, 1.0, 0.0).astype(BF)
    even = jnp.where(odd_t, 0.0, 1.0).astype(BF)
    er = lax.broadcasted_iota(jnp.int32, (E, E), 0)
    ec = lax.broadcasted_iota(jnp.int32, (E, E), 1)
    shift = jnp.where(er == lax.rem(ec + 1, E), 1.0, 0.0).astype(BF)
    home = jnp.where(er == place[...], 1.0, 0.0).astype(BF)
    member = member.astype(BF)
    loads = across(across(odd, member).astype(BF), shift) + across(
        across(even, member).astype(BF), home
    )
    load[...] = loads[:1].astype(jnp.int32)
    comb_copy.wait()
    store = []
    for q in range(B // 2):
        fetch[q].wait()
        both = [fin[2 * q + i].reshape(EM, 128) for i in range(2)]
        rows = dot(comb[...], jnp.concatenate(both, axis=1)).astype(BF)
        for i in range(2):
            for j in range(NJ):
                at = (2 * q + i) * DS + j * 128
                out[:, at : at + 128] = rows[j * T : (j + 1) * T, i * 128 : (i + 1) * 128]
            cols = slice((2 * q + i) * DS, (2 * q + i + 1) * DS)
            store.append(
                pltpu.make_async_copy(out.at[:, cols], out_hbm.at[:, cols], osem.at[2 * q + i])
            )
            store[-1].start()
    for copy in store:
        copy.wait()


def on_device(tokens, expert_ids, gate_values, placement, gate_weight, up_weight, down_weight):
    E = lax.axis_size("expert")
    B = lax.axis_size("bulk")
    T, D = tokens.shape
    TOP = expert_ids.shape[1]
    DS = gate_weight.shape[1]
    FB = gate_weight.shape[2] // B
    SL = E * CAP
    NJ = DS // 128
    MR = -(-NJ * CAP // 16) * 16
    EM = E * MR
    PAIRS = B // 2
    RG = 2 * SL
    G = FB // 256
    FH = FB // G
    KJ = -(-NJ * T // 128) * 128 // T
    spread = np.zeros((EM, SL), np.float32)
    pack = np.zeros((EM, NJ * SL), np.float32)
    for e in range(E):
        for j in range(NJ):
            for c in range(CAP):
                spread[e * MR + j * CAP + c, e * CAP + c] = 1.0
                pack[e * MR + j * CAP + c, j * SL + e * CAP + c] = 1.0
    row_tile = np.arange(EM) % MR // CAP
    row_tile = np.where(row_tile < NJ, row_tile, 2 * KJ)
    tile = row_tile[:, None] - np.arange(128)[None, :] // T
    turn = np.broadcast_to(row_tile[None, :], (T, EM))
    tables = (spread, tile, pack.T, turn, pack)
    consts = [jnp.asarray(a.astype(ml_dtypes.bfloat16)) for a in tables]
    vmem = pl.BlockSpec(memory_space=pltpu.VMEM)
    hbm = pl.BlockSpec(memory_space=pl.ANY)
    dma = pltpu.SemaphoreType.DMA
    buffers = [
        ((T, D), BF), ((TOP, T), jnp.int32), ((TOP, T), F32),
        *((a.shape, BF) for a in tables),
        ((EM, KJ * T), BF), ((B, E, MR, 128), BF), ((B, E, MR, 128), BF),
        ((PAIRS, RG, DS), BF), ((B, G, DS, 2 * FH), BF), ((B, FB, DS), BF),
        ((G, B, PAIRS, RG, 2 * FH), BF), ((G, PAIRS, PAIRS, RG, 2 * FH), BF),
        ((G, B, PAIRS, RG, 2 * FH), BF), ((B, G, PAIRS * RG, FH), BF), ((PAIRS, RG, DS), F32),
        ((B, E, MR, 128), BF), ((NJ * T, EM), BF),
    ]
    sems = [
        (8,), (2, B, G), (B,), (), (B,), (PAIRS,), (G, B, PAIRS), (G, B, PAIRS),
        (G,), (G, PAIRS, PAIRS), (B, B, G), (B, G), (B,), (PAIRS,),
    ]
    named = expert_ids.T
    fin, comb = pl.pallas_call(
        functools.partial(kernel, B, E, G),
        out_shape=(
            jax.ShapeDtypeStruct((B, E, MR, 128), BF),
            jax.ShapeDtypeStruct((NJ * T, EM), BF),
        ),
        in_specs=[hbm] * 11,
        out_specs=(hbm, hbm),
        scratch_shapes=[pltpu.VMEM(*b) for b in buffers] + [dma(n) if n else dma for n in sems],
        compiler_params=pltpu.CompilerParams(
            collective_id=0, has_side_effects=True, vmem_limit_bytes=62 * 1024 * 1024
        ),
    )(tokens, named, gate_values.T, *consts, gate_weight, up_weight, down_weight)
    return pl.pallas_call(
        close_kernel,
        out_shape=(
            jax.ShapeDtypeStruct((T, D), BF),
            jax.ShapeDtypeStruct((1, E), jnp.int32),
        ),
        in_specs=[hbm] * 4,
        out_specs=(hbm, vmem),
        scratch_shapes=[
            pltpu.VMEM((TOP, T), jnp.int32), pltpu.VMEM((1, E), jnp.int32),
            pltpu.VMEM((B, E, MR, 128), BF), pltpu.VMEM((NJ * T, EM), BF), pltpu.VMEM((T, D), BF),
            dma((PAIRS + 1,)), dma((2,)), dma((B,)),
        ],
    )(named, placement.reshape(1, E), fin, comb)


def solution(mesh):
    placed = (
        P(("bulk", "expert"), None),
        P(("bulk", "expert"), None),
        P(("bulk", "expert"), None),
        P(),
        P("expert", "bulk", None),
        P("expert", "bulk", None),
        P("expert", None, "bulk"),
    )
    return jax.shard_map(
        on_device,
        mesh=mesh,
        in_specs=placed,
        out_specs=(P(("bulk", "expert"), None), P(("bulk", "expert"), None)),
        check_vma=False,
    )
```

```python
import functools

import jax
import jax.numpy as jnp
import ml_dtypes
import numpy as np
from jax import lax
from jax.experimental import pallas as pl
from jax.experimental.pallas import tpu as pltpu
from jax.sharding import PartitionSpec as P

CAP = 3
BF = jnp.bfloat16
F32 = jnp.float32
MESH = pl.DeviceIdType.MESH


def dot(a, b):
    return jnp.dot(a, b, preferred_element_type=F32)


def across(a, b):
    return lax.dot_general(a, b, (((1,), (1,)), ((), ())), preferred_element_type=F32)


def kernel(
    B, E, G, tok_hbm, ids_hbm, gv_hbm, spread_hbm, tile_hbm, unpack_hbm, turn_hbm, pack_hbm,
    wg_hbm, wu_hbm, wd_hbm, fin, comb_hbm,
    tok, ids, gv, spread, tile, unpack, turn, pack,
    sel, og, xr, x, wgu, wd, pout, pin, prel, hin, acc, rr, comb,
    isem, wsem, dsem, osem, s1, r1, s2, r2, s3, r3, s4, r4, s5, r5,
):
    TOP, T = ids.shape
    SL = E * CAP
    DS = wg_hbm.shape[1]
    FB = wg_hbm.shape[2] // B
    FH = FB // G
    NJ = DS // 128
    MR = spread.shape[0] // E
    EM = E * MR
    PAIRS = B // 2
    RG = 2 * SL
    DC = DS if DS % 256 == 0 else 128
    mb = lax.axis_index("bulk")
    me = lax.axis_index("expert")
    pair = lax.div(mb, 2)
    is_odd = lax.rem(mb, 2)
    partner = mb + 1 - 2 * is_odd

    def wrap(i, n):
        return jnp.where(i >= n, i - n, i)

    def expert_at(k):
        return wrap(me + k, E)

    def group_at(n):
        return wrap(pair + n, PAIRS)

    def far(i):
        return wrap(2 * pair + 2 + i, B)

    def above(d):
        return jnp.where(lax.div(d, 2) > pair, 1, 0)

    def ahead(d):
        return above(d) == is_odd

    inner = jnp.where(is_odd == 1, pair < PAIRS - 1, pair > 0)
    outer = jnp.logical_not(inner)

    pairs = (
        (ids_hbm, ids), (gv_hbm, gv), (spread_hbm, spread), (tile_hbm, tile), (tok_hbm, tok),
        (unpack_hbm, unpack), (turn_hbm, turn), (pack_hbm, pack),
    )
    inputs = [pltpu.make_async_copy(a, b, isem.at[i]) for i, (a, b) in enumerate(pairs)]
    for copy in inputs[:5]:
        copy.start()
    barrier = pltpu.get_barrier_semaphore()
    for k in range(B):

        @pl.loop(0 if k else 1, E)
        def _(n):
            other = (wrap(mb + k, B), expert_at(n))
            pl.semaphore_signal(barrier, inc=1, device_id=other, device_id_type=MESH)

    for copy in inputs[5:]:
        copy.start()

    def up_copy(i, d, g):
        cols = pl.ds(pl.multiple_of(d * FB + g * FH, FH), FH)
        return pltpu.make_async_copy(
            (wg_hbm, wu_hbm)[i].at[0, :, cols],
            wgu.at[d, g, :, i * FH : (i + 1) * FH],
            wsem.at[i, d, g],
        )

    def down_copy(k):
        rows = slice(k * FB, (k + 1) * FB)
        return pltpu.make_async_copy(wd_hbm.at[0, rows, :], wd.at[k], dsem.at[k])

    def fetch_far():
        @pl.loop(0, G)
        def _(g):
            @pl.loop(0, B - 2)
            def _(n):
                for i in range(2):
                    up_copy(i, far(n), g).start()

    pl.when(outer)(fetch_far)

    for d in (partner, mb):

        @pl.loop(0, G)
        def _(g):
            for i in range(2):
                up_copy(i, d, g).start()

    pl.when(inner)(fetch_far)
    for k in range(B):
        down_copy(k).start()

    for copy in inputs[:4]:
        copy.wait()
    slot = lax.broadcasted_iota(jnp.int32, (SL, T), 0)
    slot_expert = lax.div(slot, CAP)
    slot_rank = slot - slot_expert * CAP
    named = jnp.zeros((SL, T), F32)
    gates = jnp.zeros((SL, T), F32)
    for j in range(TOP):
        hit = ids[j : j + 1, :] == slot_expert
        named = named + jnp.where(hit, 1.0, 0.0)
        gates = gates + jnp.where(hit, gv[j : j + 1, :], 0.0)
    t_row = lax.broadcasted_iota(jnp.int32, (T, T), 0)
    t_col = lax.broadcasted_iota(jnp.int32, (T, T), 1)
    before = jnp.where(t_row < t_col, 1.0, 0.0).astype(BF)
    rank = dot(named.astype(BF), before)
    chosen = jnp.where(rank == slot_rank.astype(F32), named, 0.0)

    many = 128 // T
    KJ = sel.shape[1] // T
    wide = dot(spread[...], jnp.concatenate([chosen] * many, axis=1).astype(BF))
    row_tile = tile[...].astype(F32)
    for i in range(KJ // many):
        cols = slice(i * 128, (i + 1) * 128)
        sel[:, cols] = jnp.where(row_tile == i * many, wide, 0.0).astype(BF)

    def send1(b, e):
        return pltpu.make_async_remote_copy(
            og.at[b, e], xr.at[mb, me], s1.at[b], r1.at[pair],
            device_id=(b, e), device_id_type=MESH,
        )

    def fill(q):
        stack = []
        for j in range(NJ):
            cols = [pl.ds(pl.multiple_of((2 * q + i) * DS + j * 128, 128), 128) for i in range(2)]
            stack.append(jnp.concatenate([tok[:, c] for c in cols], axis=1))
        for j in range(NJ, KJ):
            stack.append(jnp.zeros((T, 256), BF))
        rows = dot(sel[...], jnp.concatenate(stack, axis=0)).astype(BF)
        og[2 * q] = rows[:, :128].reshape(E, MR, 128)
        og[2 * q + 1] = rows[:, 128:].reshape(E, MR, 128)

    def send_near(send):
        @pl.loop(0, E)
        def _(k):
            send(partner, expert_at(k)).start()

        @pl.loop(1, E)
        def _(k):
            send(mb, expert_at(k)).start()

    def send_far(send, q):
        @pl.loop(0, E)
        def _(k):
            send(2 * q, expert_at(k)).start()
            send(2 * q + 1, expert_at(k)).start()

    inputs[4].wait()
    fill(pair)
    pl.semaphore_wait(barrier, B * E - 1)
    pltpu.make_async_copy(og.at[mb, me], xr.at[mb, me], r1.at[pair]).start()
    send_near(send1)
    for n in range(1, PAIRS):
        fill(group_at(n))
        send_far(send1, group_at(n))

    eye = jnp.where(t_row == t_col, 1.0, 0.0).astype(BF)
    weigh = across(eye, (chosen * gates).astype(BF)).astype(BF)

    comb_copy = pltpu.make_async_copy(comb, comb_hbm, osem)

    def weigh_rows():
        wide = across(weigh, spread[...])
        col_tile = turn[...].astype(F32)
        for j in range(NJ):
            comb[j * T : (j + 1) * T, :] = jnp.where(col_tile == j, wide, 0.0).astype(BF)
        comb_copy.start()

    def both(ref, q):
        return jnp.concatenate(
            [ref[2 * q].reshape(EM, 128), ref[2 * q + 1].reshape(EM, 128)], axis=1
        )

    def gather(q):
        whole = xr.at[pl.ds(2 * q, 2)]
        pltpu.make_async_copy(whole, whole, r1.at[q]).wait()
        rows = dot(unpack[...], both(xr, q))
        for j in range(NJ):
            part = rows[j * SL : (j + 1) * SL]
            x[q, :, j * 128 : (j + 1) * 128] = jnp.concatenate(
                [part[:, :128], part[:, 128:]], axis=0
            ).astype(BF)

    def partial(q, d, g, first):
        if first:
            up_copy(0, d, g).wait()
            up_copy(1, d, g).wait()
        return dot(x[q], wgu[d, g])

    def relay(d, g, q):
        return pltpu.make_async_remote_copy(
            pout.at[g, d, q], prel.at[g, d, q], s2.at[g, d, q], r2.at[g, d, q],
            device_id=(partner, me), device_id_type=MESH,
        )

    def summed(d, g, q, at):
        return pltpu.make_async_remote_copy(
            pout.at[g, d, q], pin.at[g, at, q], s2.at[g, d, q], r3.at[g, at, q],
            device_id=(d, me), device_id_type=MESH,
        )

    def direct(g):
        return pltpu.make_async_remote_copy(
            pout.at[g, partner], pin.at[g, pair], s3.at[g], r3.at[g, pair, 0],
            device_id=(partner, me), device_id_type=MESH,
        )

    def each_far(body):
        @pl.loop(0, G)
        def _(g):
            @pl.loop(0, B - 2)
            def _(i):
                body(far(i), g)

    for copy in inputs[5:]:
        copy.wait()
    for n in range(PAIRS):
        q = group_at(n)
        first, last = n == 0, n == PAIRS - 1
        if last:
            weigh_rows()
        gather(q)

        def pass_half(d, g):
            pout[g, d, q] = partial(q, d, g, first).astype(BF)
            relay(d, g, q).start()

        def pass_sum(d, g):
            own = partial(q, d, g, first)
            relay(d, g, q).wait_recv()
            pout[g, d, q] = (own + prel[g, d, q].astype(F32)).astype(BF)
            summed(d, g, q, pair).start()

        each_far(lambda d, g: pl.when(jnp.logical_not(ahead(d)))(lambda: pass_half(d, g)))

        @pl.loop(0, G)
        def _(g):
            pout[g, partner, q] = partial(q, partner, g, first).astype(BF)
            if last:
                direct(g).start()

        @pl.loop(0, G)
        def _(g):
            pout[g, mb, q] = partial(q, mb, g, first).astype(BF)

        each_far(lambda d, g: pl.when(ahead(d))(lambda: pass_sum(d, g)))

    def share(s, d, g):
        return pltpu.make_async_remote_copy(
            hin.at[s, g], hin.at[s, g], s4.at[s, d, g], r4.at[s, g],
            device_id=(d, me), device_id_type=MESH,
        )

    def opposite(d):
        return ahead(d) & (lax.rem(d, 2) == is_odd)

    def straight(d):
        return ahead(d) | (lax.rem(d, 2) != above(d))

    for g in range(G):
        direct(g).wait_recv()
        total = pout[g, mb].astype(F32) + pin[g, pair].astype(F32)
        for n in range(1, PAIRS):
            p = group_at(n)
            for q in range(PAIRS):
                summed(mb, g, q, p).wait_recv()
            total = total + pin[g, p].astype(F32)
        total = total.reshape(PAIRS * RG, 2 * FH)
        gate = total[:, :FH]
        hin[mb, g] = (
            gate / (1.0 + jnp.exp(-gate)) * total[:, FH:]
        ).astype(BF)
        share(mb, partner, g).start()
        for i in range(B - 2):
            pl.when(straight(far(i)))(lambda: share(mb, far(i), g).start())

    def add_down(s, first):
        hidden = jnp.concatenate([hin[s, g] for g in range(G)], axis=1)
        for c in range(DS // DC):
            cols = slice(c * DC, (c + 1) * DC)
            part = dot(hidden, wd[s, :, cols]).reshape(PAIRS, RG, DC)
            if first:
                acc[:, :, cols] = part
            else:
                acc[:, :, cols] += part

    for k in range(B):
        down_copy(k).wait()
    add_down(mb, True)

    for g in range(G):
        for i in range(B - 2):

            @pl.when(opposite(far(i)))
            def _():
                share(far(i), mb, g).wait_recv()
                share(far(i), partner, g).start()

    @pl.loop(0, B - 1)
    def _(j):
        turn = jnp.where(lax.rem(pair, 2) == 1, B - 2 - j, j - 1)
        s = jnp.where(j == 0, partner, far(turn))

        @pl.when((s == partner) | jnp.logical_not(opposite(s)))
        def _():
            for g in range(G):
                share(s, mb, g).wait_recv()

        add_down(s, False)

    def send5(b, e):
        return pltpu.make_async_remote_copy(
            rr.at[b, e], fin.at[mb, me], s5.at[b], r5.at[pair],
            device_id=(b, e), device_id_type=MESH,
        )

    for n in (*range(1, PAIRS), 0):
        q = group_at(n)
        stack = []
        for j in range(NJ):
            cols = slice(j * 128, (j + 1) * 128)
            stack.append(jnp.concatenate([acc[q, :SL, cols], acc[q, SL:, cols]], axis=1))
        rows = dot(pack[...], jnp.concatenate(stack, axis=0).astype(BF)).astype(BF)
        rr[2 * q] = rows[:, :128].reshape(E, MR, 128)
        rr[2 * q + 1] = rows[:, 128:].reshape(E, MR, 128)
        if n:
            send_far(send5, q)
        else:
            pltpu.make_async_copy(rr.at[mb, me], fin.at[mb, me], r5.at[pair]).start()
            send_near(send5)
    for q in range(PAIRS):
        whole = fin.at[pl.ds(2 * q, 2)]
        pltpu.make_async_copy(whole, whole, r5.at[q]).wait()

    for buf, sem in ((og, s1), (rr, s5)):
        for k in range(1, B):
            whole = buf.at[lax.rem(mb + k, B)]
            pltpu.make_async_copy(whole, whole, sem.at[lax.rem(mb + k, B)]).wait()
        rest = buf.at[mb, pl.ds(0, E - 1)]
        pltpu.make_async_copy(rest, rest, sem.at[mb]).wait()
    for g in range(G):
        direct(g).wait_send()
        share(mb, partner, g).wait_send()

        @pl.loop(0, B - 2)
        def _(i):
            d = far(i)
            pl.when(straight(d))(lambda: share(mb, d, g).wait_send())
            pl.when(opposite(d))(lambda: share(d, partner, g).wait_send())
            for q in range(PAIRS):
                relay(d, g, q).wait_send()

    comb_copy.wait()


def close_kernel(
    ids_hbm, place_hbm, fin_hbm, comb_hbm, out_hbm, load,
    ids, place, fin, comb, out, isem, nsem, osem,
):
    T = ids.shape[1]
    E = place.shape[1]
    B, _, MR, _ = fin.shape
    EM = E * MR
    NJ = comb.shape[0] // T
    DS = NJ * 128
    comb_copy = pltpu.make_async_copy(comb_hbm, comb, isem.at[0])
    comb_copy.start()
    fetch = []
    for q in range(B // 2):
        two = pl.ds(2 * q, 2)
        fetch.append(pltpu.make_async_copy(fin_hbm.at[two], fin.at[two], isem.at[q + 1]))
        fetch[-1].start()
    small = (
        pltpu.make_async_copy(ids_hbm, ids, nsem.at[0]),
        pltpu.make_async_copy(place_hbm, place, nsem.at[1]),
    )
    for copy in small:
        copy.start()
    for copy in small:
        copy.wait()
    member = jnp.zeros((E, T), F32)
    e_iota = lax.broadcasted_iota(jnp.int32, (E, T), 0)
    for j in range(ids.shape[0]):
        member = member + jnp.where(ids[j : j + 1, :] == e_iota, 1.0, 0.0)
    odd_t = lax.rem(lax.broadcasted_iota(jnp.int32, (8, T), 1), 2) == 1
    odd = jnp.where(odd_t, 1.0, 0.0).astype(BF)
    even = jnp.where(odd_t, 0.0, 1.0).astype(BF)
    er = lax.broadcasted_iota(jnp.int32, (E, E), 0)
    ec = lax.broadcasted_iota(jnp.int32, (E, E), 1)
    shift = jnp.where(er == lax.rem(ec + 1, E), 1.0, 0.0).astype(BF)
    home = jnp.where(er == place[...], 1.0, 0.0).astype(BF)
    member = member.astype(BF)
    loads = across(across(odd, member).astype(BF), shift) + across(
        across(even, member).astype(BF), home
    )
    load[...] = loads[:1].astype(jnp.int32)
    comb_copy.wait()
    store = []
    for q in range(B // 2):
        fetch[q].wait()
        both = [fin[2 * q + i].reshape(EM, 128) for i in range(2)]
        rows = dot(comb[...], jnp.concatenate(both, axis=1)).astype(BF)
        for i in range(2):
            for j in range(NJ):
                at = (2 * q + i) * DS + j * 128
                out[:, at : at + 128] = rows[j * T : (j + 1) * T, i * 128 : (i + 1) * 128]
            cols = slice((2 * q + i) * DS, (2 * q + i + 1) * DS)
            store.append(
                pltpu.make_async_copy(out.at[:, cols], out_hbm.at[:, cols], osem.at[2 * q + i])
            )
            store[-1].start()
    for copy in store:
        copy.wait()


def on_device(tokens, expert_ids, gate_values, placement, gate_weight, up_weight, down_weight):
    E = lax.axis_size("expert")
    B = lax.axis_size("bulk")
    T, D = tokens.shape
    TOP = expert_ids.shape[1]
    DS = gate_weight.shape[1]
    FB = gate_weight.shape[2] // B
    SL = E * CAP
    NJ = DS // 128
    MR = -(-NJ * CAP // 16) * 16
    EM = E * MR
    PAIRS = B // 2
    RG = 2 * SL
    G = FB // 256
    FH = FB // G
    KJ = -(-NJ * T // 128) * 128 // T
    spread = np.zeros((EM, SL), np.float32)
    pack = np.zeros((EM, NJ * SL), np.float32)
    for e in range(E):
        for j in range(NJ):
            for c in range(CAP):
                spread[e * MR + j * CAP + c, e * CAP + c] = 1.0
                pack[e * MR + j * CAP + c, j * SL + e * CAP + c] = 1.0
    row_tile = np.arange(EM) % MR // CAP
    row_tile = np.where(row_tile < NJ, row_tile, 2 * KJ)
    tile = row_tile[:, None] - np.arange(128)[None, :] // T
    turn = np.broadcast_to(row_tile[None, :], (T, EM))
    tables = (spread, tile, pack.T, turn, pack)
    consts = [jnp.asarray(a.astype(ml_dtypes.bfloat16)) for a in tables]
    vmem = pl.BlockSpec(memory_space=pltpu.VMEM)
    hbm = pl.BlockSpec(memory_space=pl.ANY)
    dma = pltpu.SemaphoreType.DMA
    buffers = [
        ((T, D), BF), ((TOP, T), jnp.int32), ((TOP, T), F32),
        *((a.shape, BF) for a in tables),
        ((EM, KJ * T), BF), ((B, E, MR, 128), BF), ((B, E, MR, 128), BF),
        ((PAIRS, RG, DS), BF), ((B, G, DS, 2 * FH), BF), ((B, FB, DS), BF),
        ((G, B, PAIRS, RG, 2 * FH), BF), ((G, PAIRS, PAIRS, RG, 2 * FH), BF),
        ((G, B, PAIRS, RG, 2 * FH), BF), ((B, G, PAIRS * RG, FH), BF), ((PAIRS, RG, DS), F32),
        ((B, E, MR, 128), BF), ((NJ * T, EM), BF),
    ]
    sems = [
        (8,), (2, B, G), (B,), (), (B,), (PAIRS,), (G, B, PAIRS), (G, B, PAIRS),
        (G,), (G, PAIRS, PAIRS), (B, B, G), (B, G), (B,), (PAIRS,),
    ]
    named = expert_ids.T
    fin, comb = pl.pallas_call(
        functools.partial(kernel, B, E, G),
        out_shape=(
            jax.ShapeDtypeStruct((B, E, MR, 128), BF),
            jax.ShapeDtypeStruct((NJ * T, EM), BF),
        ),
        in_specs=[hbm] * 11,
        out_specs=(hbm, hbm),
        scratch_shapes=[pltpu.VMEM(*b) for b in buffers] + [dma(n) if n else dma for n in sems],
        compiler_params=pltpu.CompilerParams(
            collective_id=0, has_side_effects=True, vmem_limit_bytes=62 * 1024 * 1024
        ),
    )(tokens, named, gate_values.T, *consts, gate_weight, up_weight, down_weight)
    return pl.pallas_call(
        close_kernel,
        out_shape=(
            jax.ShapeDtypeStruct((T, D), BF),
            jax.ShapeDtypeStruct((1, E), jnp.int32),
        ),
        in_specs=[hbm] * 4,
        out_specs=(hbm, vmem),
        scratch_shapes=[
            pltpu.VMEM((TOP, T), jnp.int32), pltpu.VMEM((1, E), jnp.int32),
            pltpu.VMEM((B, E, MR, 128), BF), pltpu.VMEM((NJ * T, EM), BF), pltpu.VMEM((T, D), BF),
            dma((PAIRS + 1,)), dma((2,)), dma((B,)),
        ],
    )(named, placement.reshape(1, E), fin, comb)


def solution(mesh):
    placed = (
        P(("bulk", "expert"), None),
        P(("bulk", "expert"), None),
        P(("bulk", "expert"), None),
        P(),
        P("expert", "bulk", None),
        P("expert", "bulk", None),
        P("expert", None, "bulk"),
    )
    return jax.shard_map(
        on_device,
        mesh=mesh,
        in_specs=placed,
        out_specs=(P(("bulk", "expert"), None), P(("bulk", "expert"), None)),
        check_vma=False,
    )
```
